32 devices in a mesh: grp: 2 (over x), row: 16 (over z, y, core).
Axes of the slice: x: 2, y: 2, z: 4, core: 2. Of those that a mesh axis runs over, the one named last changes fastest.
Arguments:
- facet_rows: bfloat16 [2, 16, 1024, 128], P(None, None, ('grp', 'row')), parts along dimension 2, may hold values from -6 to 6
- range_start: int32 [64], P('grp'), parts along dimension 0, may hold values from 0 to 511, as said below
- range_length: int32 [64], P('grp'), parts along dimension 0, may hold values from 128 to 256, as said below
- facet_offset: int32 [32], P('grp'), parts along dimension 0, may hold values from 0 to 511
- window_table: float32 [16, 256], replicated, may hold values from 0.25 to 1
- kernel_table: float32 [256, 8], replicated, may hold values from 0.05 to 0.5
- cell_row: int32 [64, 8192], P(('grp', 'row')), parts along dimension 0, may hold values from 0 to 248
- cell_column: int32 [64, 8192], P(('grp', 'row')), parts along dimension 0, may hold values from 0 to 248
- kernel_row: int32 [64, 8192], P(('grp', 'row')), parts along dimension 0, may hold values from 0 to 255
- kernel_column: int32 [64, 8192], P(('grp', 'row')), parts along dimension 0, may hold values from 0 to 255
Outputs:
- visibilities: float32 [2, 64, 8192], P(None, 'grp', 'row'), parts along dimension 1
The draws below stay inside these ranges and needn't reach their ends.
There are 2 independent parts, one for each index of `grp`. The reference program is written for one: setup_inputs(seed, part) draws one part's arguments, and reference() takes and returns one part's arrays. A program takes and returns all parts, laid end to end along the dimension named above; an argument that names none is the same for every part. Nothing has to cross between parts.
Inputs may be any that keep to these rules, and one draw needn't show every extreme that they name: Subgrid s is held by row index e = s // 2; its range, range_start[s] to range_start[s] + range_length[s] - 1 taken modulo 512, lies within u from e * 32 - 256 // 2 to (e + 1) * 32 + 256 // 2 - 1 modulo 512. `range_length`: ranges of uneven length.
All inputs are finite; a program needn't handle non-finite values.
Results may differ from the reference program's by a relative error of at most 0.0057.
Values may be sent and summed in bfloat16 or wider, within the bound.
A program may use at most 64 MiB of HBM per device.

```python
import math
import jax
import jax.numpy as jnp
from jax import lax

F = 16
KC = 128
SUB = 256
R_DEV = 32
SUB_DEV = 2
VPS = 8192
SUPPORT = 8
NOVER = 256
NU = 512
NSUB = 32


def range_pair(key):
    folded = jax.random.fold_in(key, 11)
    key_length, key_shift, key_first, key_second = jax.random.split(folded, 4)
    subgrid_index = jnp.arange(NSUB, dtype=jnp.int32)
    lengths = jax.random.randint(key_length, (NSUB,), SUB // 2, SUB + 1, dtype=jnp.int32)
    first_pick = jax.random.randint(key_first, (), 0, NSUB, dtype=jnp.int32)
    second_pick = (first_pick + 1 + jax.random.randint(key_second, (), 0, NSUB - 1, dtype=jnp.int32)) % NSUB
    lengths = jnp.where(subgrid_index == first_pick, SUB, lengths)
    lengths = jnp.where(subgrid_index == second_pick, SUB // 2, lengths)
    shifts = jax.random.randint(key_shift, (NSUB,), 0, R_DEV, dtype=jnp.int32)
    owners = subgrid_index // SUB_DEV
    starts = (owners * R_DEV + shifts - SUB // 2 + (SUB - lengths) // 2) % NU
    return (starts.astype(jnp.int32), lengths.astype(jnp.int32))


def draw_range_start(key, part):
    return range_pair(key)[0]


def draw_range_length(key, part):
    return range_pair(key)[1]


def set_ends(values, stream_key, least, largest):
    place = [jax.random.randint(jax.random.fold_in(stream_key, axis), (), 0, length) for axis, length in enumerate(values.shape)]
    longest = values.shape.index(max(values.shape))
    neighbour = place[:longest] + [(place[longest] + 1) % values.shape[longest]] + place[longest + 1:]
    return values.at[tuple(place)].set(least).at[tuple(neighbour)].set(largest)


def block_levels(key, shape, cuts, low, top_value):
    factor_of, own = 1.0, jax.random.fold_in(key, 6)
    for dim, shards_of in cuts:
        draws = jnp.exp(jax.random.uniform(jax.random.fold_in(own, dim), (shards_of,), jnp.float32, low / len(cuts), top_value / len(cuts)))
        factor_of = factor_of * jnp.repeat(draws, shape[dim] // shards_of).reshape([-1 if axis == dim else 1 for axis in range(len(shape))])
    return factor_of


def gaussian(stream_key, extent, scale, bound, shards=(), held_as=jnp.bfloat16):
    result = scale * jax.random.normal(stream_key, extent, jnp.float32)
    if shards:
        result = result * block_levels(stream_key, extent, shards, -0.22, 0.18)
    return jnp.clip(result, -bound, bound).astype(held_as)


def setup_inputs(seed: int = 0, part: int = 0) -> dict:
    seeds = jax.random.split(jax.random.key(seed), 11)
    part_keys = jax.random.split(jax.random.fold_in(seeds[10], part), 11)
    facet_rows = gaussian(part_keys[0], (2, F, NU, KC), 1.0, 6.0, ((2, 16),))
    range_start = draw_range_start(jax.random.fold_in(jax.random.fold_in(seeds[10], part), 71), part)
    range_length = draw_range_length(jax.random.fold_in(jax.random.fold_in(seeds[10], part), 71), part)
    facet_offset = set_ends(jax.random.randint(part_keys[3], (F,), 0, NU), jax.random.fold_in(part_keys[3], 1), 0, NU - 1).astype(jnp.int32)
    window_table = jnp.clip(jnp.exp(jax.random.uniform(seeds[4], (F, SUB), jnp.float32, math.log(0.25), math.log(1.0))), 0.25, 1.0)
    kernel_table = jnp.clip(jax.random.uniform(seeds[5], (NOVER, SUPPORT), jnp.float32, 0.05, 0.5), 0.05, 0.5)
    cell_row = set_ends(jax.random.randint(part_keys[6], (NSUB, VPS), 0, SUB - SUPPORT + 1), jax.random.fold_in(part_keys[6], 1), 0, SUB - SUPPORT).astype(jnp.int32)
    cell_column = set_ends(jax.random.randint(part_keys[7], (NSUB, VPS), 0, SUB - SUPPORT + 1), jax.random.fold_in(part_keys[7], 1), 0, SUB - SUPPORT).astype(jnp.int32)
    kernel_row = set_ends(jax.random.randint(part_keys[8], (NSUB, VPS), 0, NOVER), jax.random.fold_in(part_keys[8], 1), 0, NOVER - 1).astype(jnp.int32)
    kernel_column = set_ends(jax.random.randint(part_keys[9], (NSUB, VPS), 0, NOVER), jax.random.fold_in(part_keys[9], 1), 0, NOVER - 1).astype(jnp.int32)
    return dict(facet_rows=facet_rows, range_start=range_start, range_length=range_length, facet_offset=facet_offset, window_table=window_table, kernel_table=kernel_table, cell_row=cell_row, cell_column=cell_column, kernel_row=kernel_row, kernel_column=kernel_column)


TWO_PI = 2.0 * math.pi

def transform_table():
    kcol = jnp.arange(KC, dtype=jnp.int32)
    jcol = jnp.arange(SUB, dtype=jnp.int32)
    angles = TWO_PI * (kcol[:, None] * jcol[None, :] % SUB).astype(jnp.float32) / SUB
    scale = 1.0 / math.sqrt(KC)
    real_part = (jnp.cos(angles) * scale).astype(jnp.bfloat16)
    imag_part = (jnp.sin(angles) * scale).astype(jnp.bfloat16)
    upper = jnp.concatenate([real_part, imag_part], axis=1)
    lower = jnp.concatenate([-imag_part, real_part], axis=1)
    return jnp.concatenate([upper, lower], axis=0)

def phase_angles(offsets, positions, total_rows):
    return TWO_PI * (offsets[:, None] * positions[None, :] % total_rows).astype(jnp.float32) / total_rows

def facet_sum(gathered, window_rows, phases, inside):
    top_precision = lax.Precision.HIGHEST
    weights = window_rows * inside[None, :]
    cos_w = weights * jnp.cos(phases)
    sin_w = weights * jnp.sin(phases)
    real_out = jnp.einsum('fi,fik->ik', cos_w, gathered[0], precision=top_precision) - jnp.einsum('fi,fik->ik', sin_w, gathered[1], precision=top_precision)
    imag_out = jnp.einsum('fi,fik->ik', cos_w, gathered[1], precision=top_precision) + jnp.einsum('fi,fik->ik', sin_w, gathered[0], precision=top_precision)
    return jnp.concatenate([real_out, imag_out], axis=1)

def reference(facet_rows, range_start, range_length, facet_offset, window_table, kernel_table, cell_row, cell_column, kernel_row, kernel_column):
    top_precision = lax.Precision.HIGHEST
    facet_float = facet_rows.astype(jnp.float32)
    transform = transform_table()
    near_table = lax.optimization_barrier(kernel_table.astype(jnp.bfloat16)).astype(jnp.float32)
    kernel_taps = jnp.arange(SUPPORT, dtype=jnp.int32)
    slot_index = jnp.arange(SUB, dtype=jnp.int32)

    def one_subgrid(subgrid):
        positions = (range_start[subgrid] + slot_index) % NU
        gathered = jnp.take(facet_float, positions, axis=2)
        inside = (slot_index < range_length[subgrid]).astype(jnp.float32)
        phases = phase_angles(facet_offset, positions, NU)
        summed_rows = facet_sum(gathered, window_table, phases, inside).astype(jnp.bfloat16)
        subgrid_cells = jnp.dot(summed_rows, transform, preferred_element_type=jnp.float32).astype(jnp.bfloat16)
        subgrid_cells = lax.optimization_barrier(subgrid_cells).astype(jnp.float32)
        row_cells = cell_row[subgrid][:, None, None] + kernel_taps[None, :, None]
        col_cells = cell_column[subgrid][:, None, None] + kernel_taps[None, None, :]
        real_patch = subgrid_cells[row_cells, col_cells]
        imaginary_patch = subgrid_cells[row_cells, col_cells + SUB]
        row_weight = near_table[kernel_row[subgrid]]
        column_weight = kernel_table[kernel_column[subgrid]]
        real_visibility = jnp.einsum('tm,tc,tmc->t', row_weight, column_weight, real_patch, precision=top_precision)
        imaginary_visibility = jnp.einsum('tm,tc,tmc->t', row_weight, column_weight, imaginary_patch, precision=top_precision)
        return jnp.stack([real_visibility, imaginary_visibility])
    stacked = lax.map(one_subgrid, jnp.arange(NSUB, dtype=jnp.int32))
    return jnp.transpose(stacked, (1, 0, 2))
```

```python
import functools
import math

import jax
import jax.numpy as jnp
import numpy as np
from jax import lax
from jax.experimental import pallas as pl
from jax.experimental.pallas import tpu as pltpu
from jax.sharding import PartitionSpec as P

F = 16
KC = 128
SUB = 256
R_DEV = 32
SUB_DEV = 2
SUPPORT = 8
NOVER = 256
REACH = SUB // (2 * R_DEV)
BLOCKS = 2 * REACH + 1
LEAD = 160
TWO_PI = 2.0 * math.pi


def transform_columns():
    kcol = np.arange(KC)
    jcol = np.arange(SUB)
    angles = TWO_PI * (kcol[None, :] * jcol[:, None] % SUB) / SUB
    scale = 1.0 / math.sqrt(KC)
    real_part = np.cos(angles) * scale
    imag_part = np.sin(angles) * scale
    upper = np.concatenate([real_part, -imag_part], axis=1)
    lower = np.concatenate([imag_part, real_part], axis=1)
    parts = np.stack([upper, lower]).reshape(2, SUB // SUPPORT, SUPPORT, 2 * KC)
    tiles = parts.transpose(1, 0, 2, 3).reshape(2 * SUB, 2 * KC)
    return tiles.astype(np.float32).astype(jnp.bfloat16)


def rotated_taps(table_low, table_high, cells, picks):
    index = jnp.broadcast_to(picks, (SUPPORT, 128))
    within = index & 127
    low = jnp.take_along_axis(table_low, within, axis=1, mode="promise_in_bounds")
    high = jnp.take_along_axis(table_high, within, axis=1, mode="promise_in_bounds")
    taps = jnp.where(index < 128, low, high)
    cell = jnp.broadcast_to(cells, (SUPPORT, 128))
    for bit in (1, 2, 4):
        taps = jnp.where((cell & bit) != 0, pltpu.roll(taps, bit, axis=0), taps)
    return taps, cell


def kernel(
    devices,
    share,
    *refs,
):
    held = refs[:11]
    out_ref = refs[11]
    kept = refs[12:23]
    (
    starts_ref,
    lengths_ref,
    offset_ref,
    rows_ref,
    window_ref,
    table_ref,
    transform_ref,
    cell_row_ref,
    cell_column_ref,
    kernel_row_ref,
    kernel_column_ref,
    ) = kept
    (
    in_sem,
    turned,
    windows,
    zsend,
    zband,
    zrows,
    cells_t,
    vsend,
    vrecv,
    spreads,
    column_taps,
    column_picks,
    zs_sem,
    zr_sem,
    vs_sem,
    vr_sem,
    ) = refs[23:]
    fetches = [
        pltpu.make_async_copy(source, target, in_sem.at[number])
        for number, (source, target) in enumerate(zip(held, kept))
    ]
    for fetch in fetches:
        fetch.start()
    total_rows = R_DEV * devices
    me = lax.axis_index("row")
    barrier = pltpu.get_barrier_semaphore()

    def greet(step, carry):
        pl.semaphore_signal(
            barrier,
            inc=1,
            device_id={"row": lax.rem(me + step, devices)},
            device_id_type=pl.DeviceIdType.MESH,
        )
        return carry

    lax.fori_loop(1, devices, greet, 0)

    windows[...] = jnp.zeros_like(windows)
    zrows[:, :, BLOCKS * R_DEV :, :] = jnp.zeros((SUB_DEV, 2, SUB // 2, KC), jnp.float32)
    for fetch in fetches[:5]:
        fetch.wait()
    windows[LEAD : LEAD + SUB, :] = jnp.transpose(window_ref[...])
    lane_rows = lax.broadcasted_iota(jnp.int32, (R_DEV, F), 0)
    turns = lax.rem((me * R_DEV + lane_rows) * offset_ref[...], total_rows)
    angles = TWO_PI * turns.astype(jnp.float32) / total_rows
    cosines = jnp.cos(angles)
    sines = jnp.sin(angles)
    for facet in range(F):
        cosine = cosines[:, facet : facet + 1]
        sine = sines[:, facet : facet + 1]
        real = rows_ref[0, facet].astype(jnp.float32)
        imag = rows_ref[1, facet].astype(jnp.float32)
        turned[0, facet] = cosine * real - sine * imag
        turned[1, facet] = cosine * imag + sine * real

    def begin_of(owner, subgrid_slot):
        start = starts_ref[owner * SUB_DEV + subgrid_slot]
        begin = lax.rem(start - owner * R_DEV + SUB // 2 + total_rows, total_rows)
        return jnp.minimum(begin, LEAD)

    def block_sums(block, target):
        owner = lax.rem(me - block + REACH + devices, devices)
        for subgrid_slot in range(SUB_DEV):
            first = block * R_DEV - begin_of(owner, subgrid_slot)
            window = windows[pl.ds(first + LEAD, R_DEV), :]
            length = lengths_ref[owner * SUB_DEV + subgrid_slot]
            window = jnp.where(lane_rows + first < length, window, 0.0)
            real = jnp.zeros((R_DEV, KC), jnp.float32)
            imag = jnp.zeros((R_DEV, KC), jnp.float32)
            for facet in range(F):
                weight = window[:, facet : facet + 1]
                real = real + weight * turned[0, facet]
                imag = imag + weight * turned[1, facet]
            rows = pl.ds(subgrid_slot * R_DEV, R_DEV)
            target[block, rows, 0:KC] = real.astype(jnp.bfloat16)
            target[block, rows, KC : 2 * KC] = imag.astype(jnp.bfloat16)
        return owner

    def rows_copy(block, owner):
        return pltpu.make_async_remote_copy(
            src_ref=zsend.at[block],
            dst_ref=zband.at[block],
            send_sem=zs_sem.at[block],
            recv_sem=zr_sem.at[block],
            device_id={"row": owner},
            device_id_type=pl.DeviceIdType.MESH,
        )

    pl.semaphore_wait(barrier, devices - 1)

    def send_rows(step, carry):
        half = step // 2
        block = half + (step % 2) * (BLOCKS - 1 - 2 * half)
        owner = block_sums(block, zsend)
        rows_copy(block, owner).start()
        return carry

    lax.fori_loop(0, BLOCKS - 1, send_rows, 0)
    block_sums(REACH, zband)

    for fetch in fetches[5:]:
        fetch.wait()
    table_low = table_ref[:, 0:128]
    table_high = table_ref[:, 128:256]
    near_low = table_low.astype(jnp.bfloat16).astype(jnp.float32)
    near_high = table_high.astype(jnp.bfloat16).astype(jnp.float32)

    wide = min(256, share)
    groups = share // 128
    sub_index = lax.broadcasted_iota(jnp.int32, (SUPPORT, 128), 0)
    pair_index = lax.broadcasted_iota(jnp.int32, (2 * SUPPORT, 128), 0)

    def build(place, carry):
        for subgrid_slot in range(SUB_DEV):
            this = pl.ds(subgrid_slot, 1)
            for group in range(groups):
                lanes = pl.ds(pl.multiple_of(place * share + group * 128, 128), 128)
                piece, part = divmod(group * 128, wide)
                part = slice(part, part + 128)
                taps, cell = rotated_taps(
                    near_low, near_high, cell_row_ref[this, lanes], kernel_row_ref[this, lanes]
                )
                pair_cell = jnp.concatenate([cell, cell], axis=0)
                pair_pick = (pair_cell - pair_index + (2 * SUPPORT - 1)) >> 4
                reached = pair_pick * (2 * SUPPORT) + pair_index - pair_cell < SUPPORT
                pair_pick = jnp.where(reached, pair_pick, -1).astype(jnp.float32)
                pair_pick = pair_pick.astype(jnp.bfloat16)
                pair_taps = jnp.concatenate([taps, taps], axis=0).astype(jnp.bfloat16)
                for tile in range(SUB // (2 * SUPPORT)):
                    rows = slice(tile * 2 * SUPPORT, (tile + 1) * 2 * SUPPORT)
                    spreads[place, subgrid_slot, piece, rows, part] = jnp.where(
                        pair_pick == tile, pair_taps, jnp.zeros_like(pair_taps)
                    )
                taps, cell = rotated_taps(
                    table_low,
                    table_high,
                    cell_column_ref[this, lanes],
                    kernel_column_ref[this, lanes],
                )
                column_taps[place, subgrid_slot, piece, :, part] = taps
                column_picks[place, subgrid_slot, piece, :, part] = (
                    cell - sub_index + (SUPPORT - 1)
                ) >> 3
        return carry

    lax.fori_loop(0, devices, build, 0)

    for block in range(BLOCKS):
        if block != REACH:
            owner = lax.rem(me - block + REACH + devices, devices)
            rows_copy(block, owner).wait()
        for subgrid_slot in range(SUB_DEV):
            for part in range(2):
                zrows[subgrid_slot, part, block * R_DEV : (block + 1) * R_DEV, :] = zband[
                    block,
                    subgrid_slot * R_DEV : (subgrid_slot + 1) * R_DEV,
                    part * KC : (part + 1) * KC,
                ].astype(jnp.float32)
    for subgrid_slot in range(SUB_DEV):
        rows = pl.ds(begin_of(me, subgrid_slot), SUB)
        own_rows = jnp.concatenate(
            [zrows[subgrid_slot, 0, rows, :], zrows[subgrid_slot, 1, rows, :]], axis=1
        )
        cells_t[subgrid_slot] = lax.dot_general(
            transform_ref[...],
            own_rows.astype(jnp.bfloat16),
            (((1,), (1,)), ((), ())),
            preferred_element_type=jnp.float32,
        ).astype(jnp.bfloat16)

    def slots_copy(place, source, target):
        return pltpu.make_async_remote_copy(
            src_ref=vsend.at[source],
            dst_ref=vrecv.at[target],
            send_sem=vs_sem.at[source],
            recv_sem=vr_sem.at[target],
            device_id={"row": place},
            device_id_type=pl.DeviceIdType.MESH,
        )

    def degrid(step, carry):
        place = lax.rem(me + step, devices)
        for subgrid_slot in range(SUB_DEV):
            for piece in range(share // wide):
                column_pick = column_picks[place, subgrid_slot, piece]
                column_tap = column_taps[place, subgrid_slot, piece]
                along = jnp.dot(
                    cells_t[subgrid_slot],
                    spreads[place, subgrid_slot, piece],
                    preferred_element_type=jnp.float32,
                )
                real = along[0:SUPPORT]
                imag = along[SUPPORT : 2 * SUPPORT]
                for tile in range(1, SUB // SUPPORT):
                    chosen = column_pick == tile
                    low = 2 * tile * SUPPORT
                    real = jnp.where(chosen, along[low : low + SUPPORT], real)
                    imag = jnp.where(chosen, along[low + SUPPORT : low + 2 * SUPPORT], imag)
                real = jnp.sum(real * column_tap, axis=0, keepdims=True)
                imag = jnp.sum(imag * column_tap, axis=0, keepdims=True)
                for group in range(wide // 128):
                    row = piece * (wide // 128) + group
                    part = slice(group * 128, (group + 1) * 128)
                    first = subgrid_slot * groups + row
                    vsend[place, first : first + 1, :] = real[:, part]
                    first = (SUB_DEV + subgrid_slot) * groups + row
                    vsend[place, first : first + 1, :] = imag[:, part]

        @pl.when(step < devices)
        def _():
            slots_copy(place, place, me).start()

        return carry

    lax.fori_loop(1, devices + 1, degrid, 0)
    vrecv[me] = vsend[me]

    def settle(step, carry):
        place = lax.rem(me + step, devices)
        slots_copy(place, place, place).wait()
        return carry

    lax.fori_loop(1, devices, settle, 0)
    for place in range(devices):
        for part in range(2):
            for subgrid_slot in range(SUB_DEV):
                for group in range(groups):
                    first = (part * SUB_DEV + subgrid_slot) * groups + group
                    row = place * SUB_DEV + subgrid_slot
                    out_ref[part, row : row + 1, group * 128 : (group + 1) * 128] = vrecv[
                        place, first : first + 1, :
                    ]


def local(
    facet_rows,
    range_start,
    range_length,
    facet_offset,
    window_table,
    kernel_table,
    cell_row,
    cell_column,
    kernel_row,
    kernel_column,
):
    devices = lax.axis_size("row")
    visibilities = cell_row.shape[1]
    share = visibilities // devices
    wide = min(256, share)
    pieces = (devices, SUB_DEV, share // wide)
    sent_rows = 2 * SUB_DEV * share // 128
    vmem = pl.BlockSpec(memory_space=pltpu.VMEM)
    hbm = pl.BlockSpec(memory_space=pltpu.HBM)
    operands = (
        range_start,
        range_length,
        facet_offset.reshape(1, F),
        facet_rows,
        window_table,
        kernel_table.T,
        jnp.asarray(transform_columns()),
        cell_row,
        cell_column,
        kernel_row,
        kernel_column,
    )
    return pl.pallas_call(
        functools.partial(kernel, devices, share),
        out_shape=pltpu.VMEM((2, SUB_DEV * devices, share), jnp.float32),
        in_specs=[hbm] * 11,
        out_specs=vmem,
        scratch_shapes=[
            (pltpu.SMEM if number < 2 else pltpu.VMEM)(value.shape, value.dtype)
            for number, value in enumerate(operands)
        ]
        + [
            pltpu.SemaphoreType.DMA((11,)),
            pltpu.VMEM((2, F, R_DEV, KC), jnp.float32),
            pltpu.VMEM((LEAD + SUB + R_DEV, F), jnp.float32),
            pltpu.VMEM((BLOCKS, SUB_DEV * R_DEV, 2 * KC), jnp.bfloat16),
            pltpu.VMEM((BLOCKS, SUB_DEV * R_DEV, 2 * KC), jnp.bfloat16),
            pltpu.VMEM((SUB_DEV, 2, BLOCKS * R_DEV + SUB // 2, KC), jnp.float32),
            pltpu.VMEM((SUB_DEV, 2 * SUB, SUB), jnp.bfloat16),
            pltpu.VMEM((devices, sent_rows, 128), jnp.float32),
            pltpu.VMEM((devices, sent_rows, 128), jnp.float32),
            pltpu.VMEM(pieces + (SUB, wide), jnp.bfloat16),
            pltpu.VMEM(pieces + (SUPPORT, wide), jnp.float32),
            pltpu.VMEM(pieces + (SUPPORT, wide), jnp.int32),
            pltpu.SemaphoreType.DMA((BLOCKS,)),
            pltpu.SemaphoreType.DMA((BLOCKS,)),
            pltpu.SemaphoreType.DMA((devices,)),
            pltpu.SemaphoreType.DMA((devices,)),
        ],
        compiler_params=pltpu.CompilerParams(
            collective_id=0, has_side_effects=True, vmem_limit_bytes=25165824
        ),
        name="extract_and_degrid",
    )(*[pltpu.with_memory_space_constraint(o, pltpu.HBM) for o in operands])


def solution(mesh):
    placed = (
        P(None, None, ("grp", "row"), None),
        P("grp"),
        P("grp"),
        P("grp"),
        P(),
        P(),
        P(("grp", "row"), None),
        P(("grp", "row"), None),
        P(("grp", "row"), None),
        P(("grp", "row"), None),
    )
    return jax.shard_map(
        local, mesh=mesh, in_specs=placed, out_specs=P(None, "grp", "row"), check_vma=False
    )
```

```python
import functools
import math

import jax
import jax.numpy as jnp
import numpy as np
from jax import lax
from jax.experimental import pallas as pl
from jax.experimental.pallas import tpu as pltpu
from jax.sharding import PartitionSpec as P

F = 16
KC = 128
SUB = 256
R_DEV = 32
SUB_DEV = 2
SUPPORT = 8
NOVER = 256
REACH = SUB // (2 * R_DEV)
BLOCKS = 2 * REACH + 1
LEAD = 160
PLANE = 4
UNROLL = 3
TWO_PI = 2.0 * math.pi


def transform_columns():
    kcol = np.arange(KC)
    jcol = np.arange(SUB)
    angles = TWO_PI * (kcol[None, :] * jcol[:, None] % SUB) / SUB
    scale = 1.0 / math.sqrt(KC)
    real_part = np.cos(angles) * scale
    imag_part = np.sin(angles) * scale
    upper = np.concatenate([real_part, -imag_part], axis=1)
    lower = np.concatenate([imag_part, real_part], axis=1)
    parts = np.stack([upper, lower]).reshape(2, SUB // SUPPORT, SUPPORT, 2 * KC)
    tiles = parts.transpose(1, 0, 2, 3).reshape(2 * SUB, 2 * KC)
    return tiles.astype(np.float32).astype(jnp.bfloat16)


def rotated_taps(table_low, table_high, cells, picks, turn=0):
    index = jnp.broadcast_to(picks, (SUPPORT, 128))
    within = index & 127
    low = jnp.take_along_axis(table_low, within, axis=1, mode="promise_in_bounds")
    high = jnp.take_along_axis(table_high, within, axis=1, mode="promise_in_bounds")
    taps = jnp.where(index < 128, low, high)
    cell = (jnp.broadcast_to(cells, (SUPPORT, 128)) + turn) & (SUB - 1)
    for bit in (1, 2, 4):
        taps = jnp.where((cell & bit) != 0, pltpu.roll(taps, bit, axis=0), taps)
    return taps, cell


def kernel(
    devices,
    share,
    *refs,
):
    held = refs[:11]
    out_ref = refs[11]
    kept = refs[12:23]
    (
    starts_ref,
    lengths_ref,
    offset_ref,
    window_ref,
    rows_ref,
    table_ref,
    transform_ref,
    cell_row_ref,
    cell_column_ref,
    kernel_row_ref,
    kernel_column_ref,
    ) = kept
    (
    in_sem,
    windows,
    zsend,
    zband,
    cells_t,
    found,
    vsend,
    vrecv,
    spreads,
    column_taps,
    column_picks,
    zs_sem,
    zr_sem,
    vs_sem,
    vr_sem,
    ) = refs[23:]
    fetches = [
        pltpu.make_async_copy(source, target, in_sem.at[number])
        for number, (source, target) in enumerate(zip(held, kept))
    ]
    for fetch in fetches:
        fetch.start()
    total_rows = R_DEV * devices
    me = lax.axis_index("row")
    barrier = pltpu.get_barrier_semaphore()

    def greet(step, carry):
        pl.semaphore_signal(
            barrier,
            inc=1,
            device_id={"row": lax.rem(me + step, devices)},
            device_id_type=pl.DeviceIdType.MESH,
        )
        return carry

    lax.fori_loop(1, devices, greet, 0)

    windows[:, 0:LEAD, :] = jnp.zeros((F // 4, LEAD, 128), jnp.float32)
    windows[:, LEAD + SUB :, :] = jnp.zeros((F // 4, R_DEV, 128), jnp.float32)
    for fetch in fetches[:4]:
        fetch.wait()
    for tile in range(F // 4):
        repeated = jnp.concatenate(
            [
                jnp.broadcast_to(window_ref[facet : facet + 1, :], (R_DEV, SUB))
                for facet in range(4 * tile, 4 * tile + 4)
            ],
            axis=0,
        )
        windows[tile, LEAD : LEAD + SUB, :] = jnp.transpose(repeated)
    lanes8 = lax.broadcasted_iota(jnp.int32, (8, 128), 1)
    tiles8 = lax.broadcasted_iota(jnp.int32, (8, 128), 0)
    facets8 = tiles8 * 4 + lanes8 // R_DEV
    offsets = jnp.zeros((8, 128), jnp.int32)
    for facet in range(F):
        offsets = jnp.where(facets8 == facet, offset_ref[facet], offsets)
    turns = lax.rem((me * R_DEV + lanes8 % R_DEV) * offsets, total_rows)
    angles = TWO_PI * turns.astype(jnp.float32) / total_rows
    lane_rows = lax.broadcasted_iota(jnp.int32, (R_DEV, 128), 0)
    lane_slots = lax.broadcasted_iota(jnp.int32, (R_DEV, 128), 1) % R_DEV
    diagonal = lane_rows == lane_slots

    def spread_out(values):
        return jnp.concatenate(
            [
                jnp.where(diagonal, jnp.broadcast_to(values[t : t + 1, :], (R_DEV, 128)), 0.0)
                for t in range(F // 4)
            ],
            axis=1,
        )

    cosines = spread_out(jnp.cos(angles))
    sines = spread_out(jnp.sin(angles))
    fetches[4].wait()
    held_rows = jnp.concatenate(
        [rows_ref[0].reshape(F * R_DEV, KC), rows_ref[1].reshape(F * R_DEV, KC)], axis=1
    )

    def begin_of(owner, subgrid_slot):
        start = starts_ref[owner * SUB_DEV + subgrid_slot]
        begin = lax.rem(start - owner * R_DEV + SUB // 2 + total_rows, total_rows)
        return jnp.minimum(begin, LEAD)

    def owner_of(block):
        return lax.rem(me - block + REACH + devices, devices)

    def block_sums(subgrid_slot):
        weights = []
        for block in range(BLOCKS):
            first = block * R_DEV - begin_of(owner_of(block), subgrid_slot)
            window = jnp.concatenate(
                [windows[t, pl.ds(first + LEAD, R_DEV), :] for t in range(F // 4)], axis=1
            )
            weights.append((window * cosines).astype(jnp.bfloat16))
            weights.append((window * sines).astype(jnp.bfloat16))
        sums = jnp.dot(
            jnp.concatenate(weights, axis=0), held_rows, preferred_element_type=jnp.float32
        )
        for block in range(BLOCKS):
            owner = owner_of(block)
            first = block * R_DEV - begin_of(owner, subgrid_slot)
            inside = lane_rows + first < lengths_ref[owner * SUB_DEV + subgrid_slot]
            low = block * 2 * R_DEV
            by_cosine = sums[low : low + R_DEV]
            by_sine = sums[low + R_DEV : low + 2 * R_DEV]
            real = jnp.where(inside, by_cosine[:, 0:KC] - by_sine[:, KC:], 0.0)
            imag = jnp.where(inside, by_cosine[:, KC:] + by_sine[:, 0:KC], 0.0)
            target = zband if block == REACH else zsend
            target[subgrid_slot, block, :, 0:KC] = real.astype(jnp.bfloat16)
            target[subgrid_slot, block, :, KC : 2 * KC] = imag.astype(jnp.bfloat16)

    def rows_copy(subgrid_slot, block):
        return pltpu.make_async_remote_copy(
            src_ref=zsend.at[subgrid_slot, block],
            dst_ref=zband.at[subgrid_slot, block],
            send_sem=zs_sem.at[subgrid_slot, block],
            recv_sem=zr_sem.at[subgrid_slot, block],
            device_id={"row": owner_of(block)},
            device_id_type=pl.DeviceIdType.MESH,
        )

    far_first = sorted((b for b in range(BLOCKS) if b != REACH), key=lambda b: -abs(b - REACH))
    block_sums(0)
    pl.semaphore_wait(barrier, devices - 1)
    for block in far_first:
        rows_copy(0, block).start()
    block_sums(1)

    for fetch in fetches[5:]:
        fetch.wait()
    table_low = table_ref[:, 0:128]
    table_high = table_ref[:, 128:256]
    near_low = table_low.astype(jnp.bfloat16).astype(jnp.float32)
    near_high = table_high.astype(jnp.bfloat16).astype(jnp.float32)

    wide = min(256, share)
    groups = share // 128
    sub_index = lax.broadcasted_iota(jnp.int32, (SUPPORT, 128), 0)
    pair_index = lax.broadcasted_iota(jnp.int32, (2 * SUPPORT, 128), 0)

    def build(subgrid_slot, place):
        this = pl.ds(subgrid_slot, 1)
        for group in range(groups):
            lanes = pl.ds(pl.multiple_of(place * share + group * 128, 128), 128)
            piece, part = divmod(group * 128, wide)
            part = slice(part, part + 128)
            taps, cell = rotated_taps(
                near_low,
                near_high,
                cell_row_ref[this, lanes],
                kernel_row_ref[this, lanes],
                begin_of(me, subgrid_slot),
            )
            pair_cell = jnp.concatenate([cell, cell], axis=0)
            pair_pick = (pair_cell - pair_index + (2 * SUPPORT - 1)) >> 4
            reached = pair_pick * (2 * SUPPORT) + pair_index - pair_cell < SUPPORT
            pair_pick = jnp.where(reached, pair_pick & (SUB // (2 * SUPPORT) - 1), -1).astype(jnp.float32)
            pair_pick = pair_pick.astype(jnp.bfloat16)
            pair_taps = jnp.concatenate([taps, taps], axis=0).astype(jnp.bfloat16)
            for tile in range(SUB // (2 * SUPPORT)):
                rows = slice(tile * 2 * SUPPORT, (tile + 1) * 2 * SUPPORT)
                spreads[place, subgrid_slot, piece, rows, part] = jnp.where(
                    pair_pick == tile, pair_taps, jnp.zeros_like(pair_taps)
                )
            taps, cell = rotated_taps(
                table_low,
                table_high,
                cell_column_ref[this, lanes],
                kernel_column_ref[this, lanes],
            )
            column_taps[place, subgrid_slot, piece, :, part] = taps
            column_picks[place, subgrid_slot, piece, :, part] = (
                cell - sub_index + (SUPPORT - 1)
            ) >> 3

    def build_one(subgrid_slot):
        def step(place, carry):
            build(subgrid_slot, place)
            return carry

        lax.fori_loop(0, devices, step, 0, unroll=2)

    build_one(0)
    for block in far_first:
        rows_copy(1, block).start()
    build_one(1)

    def transform(subgrid_slot):
        for block in range(BLOCKS):
            if block != REACH:
                rows_copy(subgrid_slot, block).wait()
        parts = [zband[subgrid_slot, block] for block in range(BLOCKS - 1)]
        parts[0] = parts[0] + zband[subgrid_slot, BLOCKS - 1]
        cells_t[subgrid_slot] = lax.dot_general(
            transform_ref[...],
            jnp.concatenate(parts, axis=0),
            (((1,), (1,)), ((), ())),
            preferred_element_type=jnp.float32,
        ).astype(jnp.bfloat16)

    def slots_copy(place, source, target):
        return pltpu.make_async_remote_copy(
            src_ref=vsend.at[source],
            dst_ref=vrecv.at[target],
            send_sem=vs_sem.at[source],
            recv_sem=vr_sem.at[target],
            device_id={"row": place},
            device_id_type=pl.DeviceIdType.MESH,
        )

    planes = devices // PLANE

    def place_of(turn, spin):
        here = me // PLANE
        upper = here >= planes // 2
        near = jnp.where(upper, planes - 1 - here, here)
        plane = planes - turn
        plane = jnp.where(plane > near, plane, plane - 1)
        plane = jnp.where(turn == planes, near, plane)
        plane = jnp.where(upper, planes - 1 - plane, plane)
        core = me % 2
        side = me % PLANE // 2
        side = 1 - side if spin < 2 else side
        core = core if spin % 2 else 1 - core
        return plane * PLANE + side * 2 + core

    def degrid(subgrid_slot, place):
        for piece in range(share // wide):
            column_pick = column_picks[place, subgrid_slot, piece]
            column_tap = column_taps[place, subgrid_slot, piece]
            along = jnp.dot(
                cells_t[subgrid_slot],
                spreads[place, subgrid_slot, piece],
                preferred_element_type=jnp.float32,
            )
            real = along[0:SUPPORT]
            imag = along[SUPPORT : 2 * SUPPORT]
            for tile in range(1, SUB // SUPPORT):
                chosen = column_pick == tile
                low = 2 * tile * SUPPORT
                real = jnp.where(chosen, along[low : low + SUPPORT], real)
                imag = jnp.where(chosen, along[low + SUPPORT : low + 2 * SUPPORT], imag)
            real = jnp.sum(real * column_tap, axis=0, keepdims=True)
            imag = jnp.sum(imag * column_tap, axis=0, keepdims=True)
            for group in range(wide // 128):
                row = piece * (wide // 128) + group
                part = slice(group * 128, (group + 1) * 128)
                first = subgrid_slot * groups + row
                found[place, first : first + 1, :] = real[:, part]
                first = (SUB_DEV + subgrid_slot) * groups + row
                found[place, first : first + 1, :] = imag[:, part]

    def send_slots(places):
        for place in places:
            vsend[place] = found[place].astype(jnp.bfloat16)
        for place in places:
            slots_copy(place, place, me).start()

    def first_pass(turn, carry):
        for spin in range(PLANE):
            degrid(0, place_of(turn, spin))
        return carry

    def second_pass(pair, carry):
        places = [
            place_of(2 * pair + turn, spin) for turn in (1, 2) for spin in range(PLANE)
        ]
        for place in places:
            degrid(1, place)
        send_slots(places)
        return carry

    transform(0)
    lax.fori_loop(1, planes, first_pass, 0, unroll=UNROLL)
    for spin in range(2):
        degrid(0, place_of(planes, spin))
    transform(1)
    lax.fori_loop(0, (planes - 2) // 2, second_pass, 0)
    nearer = [place_of(planes - 1, spin) for spin in range(PLANE)]
    nearer += [place_of(planes, spin) for spin in range(2)]
    for place in nearer:
        degrid(1, place)
    send_slots(nearer)
    beside = place_of(planes, 2)
    for subgrid_slot in range(SUB_DEV):
        degrid(subgrid_slot, beside)
        degrid(subgrid_slot, me)
    send_slots([beside])
    vrecv[me] = found[me].astype(jnp.bfloat16)

    def settle(step, carry):
        place = lax.rem(me + step, devices)
        slots_copy(place, place, place).wait()
        return carry

    lax.fori_loop(1, devices, settle, 0)
    for place in range(devices):
        taken = vrecv[place].astype(jnp.float32)
        for part in range(2):
            for subgrid_slot in range(SUB_DEV):
                for group in range(groups):
                    first = (part * SUB_DEV + subgrid_slot) * groups + group
                    row = place * SUB_DEV + subgrid_slot
                    out_ref[part, row : row + 1, group * 128 : (group + 1) * 128] = taken[
                        first : first + 1, :
                    ]


def local(
    facet_rows,
    range_start,
    range_length,
    facet_offset,
    window_table,
    kernel_table,
    cell_row,
    cell_column,
    kernel_row,
    kernel_column,
):
    devices = lax.axis_size("row")
    visibilities = cell_row.shape[1]
    share = visibilities // devices
    wide = min(256, share)
    pieces = (devices, SUB_DEV, share // wide)
    sent_rows = -(-2 * SUB_DEV * share // 128 // 16) * 16
    vmem = pl.BlockSpec(memory_space=pltpu.VMEM)
    hbm = pl.BlockSpec(memory_space=pltpu.HBM)
    operands = (
        range_start,
        range_length,
        facet_offset,
        window_table,
        facet_rows,
        kernel_table.T,
        jnp.asarray(transform_columns()),
        cell_row,
        cell_column,
        kernel_row,
        kernel_column,
    )
    return pl.pallas_call(
        functools.partial(kernel, devices, share),
        out_shape=pltpu.VMEM((2, SUB_DEV * devices, share), jnp.float32),
        in_specs=[hbm] * 11,
        out_specs=vmem,
        scratch_shapes=[
            (pltpu.SMEM if number < 3 else pltpu.VMEM)(value.shape, value.dtype)
            for number, value in enumerate(operands)
        ]
        + [
            pltpu.SemaphoreType.DMA((11,)),
            pltpu.VMEM((F // 4, LEAD + SUB + R_DEV, 128), jnp.float32),
            pltpu.VMEM((SUB_DEV, BLOCKS, R_DEV, 2 * KC), jnp.bfloat16),
            pltpu.VMEM((SUB_DEV, BLOCKS, R_DEV, 2 * KC), jnp.bfloat16),
            pltpu.VMEM((SUB_DEV, 2 * SUB, SUB), jnp.bfloat16),
            pltpu.VMEM((devices, sent_rows, 128), jnp.float32),
            pltpu.VMEM((devices, sent_rows, 128), jnp.bfloat16),
            pltpu.VMEM((devices, sent_rows, 128), jnp.bfloat16),
            pltpu.VMEM(pieces + (SUB, wide), jnp.bfloat16),
            pltpu.VMEM(pieces + (SUPPORT, wide), jnp.float32),
            pltpu.VMEM(pieces + (SUPPORT, wide), jnp.int32),
            pltpu.SemaphoreType.DMA((SUB_DEV, BLOCKS)),
            pltpu.SemaphoreType.DMA((SUB_DEV, BLOCKS)),
            pltpu.SemaphoreType.DMA((devices,)),
            pltpu.SemaphoreType.DMA((devices,)),
        ],
        compiler_params=pltpu.CompilerParams(
            collective_id=0, has_side_effects=True, vmem_limit_bytes=25165824
        ),
        name="extract_and_degrid",
    )(*[pltpu.with_memory_space_constraint(o, pltpu.HBM) for o in operands])


def solution(mesh):
    placed = (
        P(None, None, ("grp", "row"), None),
        P("grp"),
        P("grp"),
        P("grp"),
        P(),
        P(),
        P(("grp", "row"), None),
        P(("grp", "row"), None),
        P(("grp", "row"), None),
        P(("grp", "row"), None),
    )
    return jax.shard_map(
        local, mesh=mesh, in_specs=placed, out_specs=P(None, "grp", "row"), check_vma=False
    )
```

```python
import functools
import math

import jax
import jax.numpy as jnp
import numpy as np
from jax import lax
from jax.experimental import pallas as pl
from jax.experimental.pallas import tpu as pltpu
from jax.sharding import PartitionSpec as P

F = 16
KC = 128
SUB = 256
R_DEV = 32
SUB_DEV = 2
SUPPORT = 8
NOVER = 256
REACH = SUB // (2 * R_DEV)
BLOCKS = 2 * REACH + 1
LEAD = 160
PLANE = 4
UNROLL = 3
BUILT = 8
TWO_PI = 2.0 * math.pi


def transform_rows():
    kcol = np.arange(KC)
    jcol = np.arange(SUB)
    angles = TWO_PI * (kcol[:, None] * jcol[None, :] % SUB) / SUB
    scale = 1.0 / math.sqrt(KC)
    parts = np.stack([np.cos(angles) * scale, np.sin(angles) * scale])
    tiles = parts.reshape(2, KC // SUPPORT, SUPPORT, SUB).transpose(1, 0, 2, 3)
    return tiles.reshape(2 * KC, SUB).astype(np.float32).astype(jnp.bfloat16)


def spread_taps(tables, cells, picks, turn):
    index = jnp.broadcast_to(picks, (SUPPORT, 128))
    within = index & 127
    low, high = (
        jnp.take_along_axis(table, within, axis=1, mode="promise_in_bounds") for table in tables
    )
    taps = jnp.where(index < 128, low, high)
    cell = jnp.broadcast_to(cells + turn, (SUPPORT, 128))
    for bit in (1, 2, 4):
        taps = jnp.where((cell & bit) != 0, pltpu.roll(taps, bit, axis=0), taps)
    row = lax.broadcasted_iota(jnp.int32, (SUPPORT, 128), 0)
    pick = (((cell + (SUPPORT - 1 - row)) >> 3) & (SUB // SUPPORT - 1)).astype(jnp.float32)
    pair_pick = jnp.concatenate([pick, pick - 1.0], axis=0).astype(jnp.bfloat16)
    pair_taps = jnp.concatenate([taps, taps], axis=0).astype(jnp.bfloat16)
    parts = [
        jnp.where(pair_pick == tile, pair_taps, jnp.zeros_like(pair_taps))
        for tile in range(0, SUB // SUPPORT, 2)
    ]
    return jnp.concatenate(parts, axis=0)


def kernel(
    devices,
    share,
    *refs,
):
    held = refs[:11]
    out_ref = refs[11]
    kept = refs[12:23]
    (
    starts_ref,
    lengths_ref,
    offset_ref,
    window_ref,
    rows_ref,
    table_ref,
    transform_ref,
    cell_row_ref,
    cell_column_ref,
    kernel_row_ref,
    kernel_column_ref,
    ) = kept
    (
    in_sem,
    windows,
    zsend,
    zband,
    turned,
    found,
    vsend,
    vrecv,
    spreads,
    factors,
    zs_sem,
    zr_sem,
    vs_sem,
    vr_sem,
    ) = refs[23:]
    fetches = [
        pltpu.make_async_copy(source, target, in_sem.at[number])
        for number, (source, target) in enumerate(zip(held, kept))
    ]
    for fetch in fetches:
        fetch.start()
    total_rows = R_DEV * devices
    me = lax.axis_index("row")
    barrier = pltpu.get_barrier_semaphore()

    def greet(step, carry):
        pl.semaphore_signal(
            barrier,
            inc=1,
            device_id={"row": lax.rem(me + step, devices)},
            device_id_type=pl.DeviceIdType.MESH,
        )
        return carry

    lax.fori_loop(1, devices, greet, 0)

    windows[:, 0:LEAD, :] = jnp.zeros((F // 4, LEAD, 128), jnp.float32)
    windows[:, LEAD + SUB :, :] = jnp.zeros((F // 4, R_DEV, 128), jnp.float32)
    for fetch in fetches[:4]:
        fetch.wait()
    for tile in range(F // 4):
        repeated = jnp.concatenate(
            [
                jnp.broadcast_to(window_ref[facet : facet + 1, :], (R_DEV, SUB))
                for facet in range(4 * tile, 4 * tile + 4)
            ],
            axis=0,
        )
        windows[tile, LEAD : LEAD + SUB, :] = jnp.transpose(repeated)
    lanes8 = lax.broadcasted_iota(jnp.int32, (8, 128), 1)
    tiles8 = lax.broadcasted_iota(jnp.int32, (8, 128), 0)
    facets8 = tiles8 * 4 + lanes8 // R_DEV
    offsets = jnp.zeros((8, 128), jnp.int32)
    for facet in range(F):
        offsets = jnp.where(facets8 == facet, offset_ref[facet], offsets)
    turns = lax.rem((me * R_DEV + lanes8 % R_DEV) * offsets, total_rows)
    angles = TWO_PI * turns.astype(jnp.float32) / total_rows
    lane_rows = lax.broadcasted_iota(jnp.int32, (R_DEV, 128), 0)
    lane_slots = lax.broadcasted_iota(jnp.int32, (R_DEV, 128), 1) % R_DEV
    diagonal = lane_rows == lane_slots

    def spread_out(values):
        return jnp.concatenate(
            [
                jnp.where(diagonal, jnp.broadcast_to(values[t : t + 1, :], (R_DEV, 128)), 0.0)
                for t in range(F // 4)
            ],
            axis=1,
        )

    cosines = spread_out(jnp.cos(angles))
    sines = spread_out(jnp.sin(angles))
    fetches[4].wait()
    held_rows = jnp.concatenate(
        [rows_ref[0].reshape(F * R_DEV, KC), rows_ref[1].reshape(F * R_DEV, KC)], axis=1
    )

    def begin_of(owner, subgrid_slot):
        start = starts_ref[owner * SUB_DEV + subgrid_slot]
        begin = lax.rem(start - owner * R_DEV + SUB // 2 + total_rows, total_rows)
        return jnp.minimum(begin, LEAD)

    def owner_of(block):
        return lax.rem(me - block + REACH + devices, devices)

    def block_sums(subgrid_slot):
        weights = []
        for block in range(BLOCKS):
            first = block * R_DEV - begin_of(owner_of(block), subgrid_slot)
            window = jnp.concatenate(
                [windows[t, pl.ds(first + LEAD, R_DEV), :] for t in range(F // 4)], axis=1
            )
            weights.append((window * cosines).astype(jnp.bfloat16))
            weights.append((window * sines).astype(jnp.bfloat16))
        sums = jnp.dot(
            jnp.concatenate(weights, axis=0), held_rows, preferred_element_type=jnp.float32
        )
        for block in range(BLOCKS):
            owner = owner_of(block)
            first = block * R_DEV - begin_of(owner, subgrid_slot)
            inside = lane_rows + first < lengths_ref[owner * SUB_DEV + subgrid_slot]
            low = block * 2 * R_DEV
            by_cosine = sums[low : low + R_DEV]
            by_sine = sums[low + R_DEV : low + 2 * R_DEV]
            real = jnp.where(inside, by_cosine[:, 0:KC] - by_sine[:, KC:], 0.0)
            imag = jnp.where(inside, by_cosine[:, KC:] + by_sine[:, 0:KC], 0.0)
            target = zband if block == REACH else zsend
            target[subgrid_slot, block, :, 0:KC] = real.astype(jnp.bfloat16)
            target[subgrid_slot, block, :, KC : 2 * KC] = imag.astype(jnp.bfloat16)

    def rows_copy(subgrid_slot, block):
        return pltpu.make_async_remote_copy(
            src_ref=zsend.at[subgrid_slot, block],
            dst_ref=zband.at[subgrid_slot, block],
            send_sem=zs_sem.at[subgrid_slot, block],
            recv_sem=zr_sem.at[subgrid_slot, block],
            device_id={"row": owner_of(block)},
            device_id_type=pl.DeviceIdType.MESH,
        )

    far_first = sorted((b for b in range(BLOCKS) if b != REACH), key=lambda b: -abs(b - REACH))
    block_sums(0)
    pl.semaphore_wait(barrier, devices - 1)
    for block in far_first:
        rows_copy(0, block).start()
    block_sums(1)

    for fetch in fetches[5:]:
        fetch.wait()
    table_low = table_ref[:, 0:128]
    table_high = table_ref[:, 128:256]
    tables = [
        part.astype(jnp.bfloat16).astype(jnp.float32) for part in (table_low, table_high)
    ]

    wide = min(256, share)
    groups = share // 128

    def build(subgrid_slot, place):
        this = pl.ds(subgrid_slot, 1)
        for piece in range(share // wide):
            lanes = [
                pl.ds(pl.multiple_of(place * share + piece * wide + at, 128), 128)
                for at in range(0, wide, 128)
            ]
            columns = [
                spread_taps(tables, cell_column_ref[this, at], kernel_column_ref[this, at], 0)
                for at in lanes
            ]
            factors[place, subgrid_slot, piece] = jnp.dot(
                transform_ref[...],
                jnp.concatenate(columns, axis=1),
                preferred_element_type=jnp.float32,
            )
            begin = begin_of(me, subgrid_slot)
            for group, at in enumerate(lanes):
                spreads[place, subgrid_slot, piece, group] = spread_taps(
                    tables, cell_row_ref[this, at], kernel_row_ref[this, at], begin
                )

    def build_some(subgrid_slot, low, high):
        def step(number, carry):
            for place in range(BUILT):
                build(subgrid_slot, number * BUILT + place)
            return carry

        lax.fori_loop(low // BUILT, high // BUILT, step, 0)

    build_some(0, 0, devices // 2)
    for block in far_first:
        rows_copy(1, block).start()
    build_some(0, devices // 2, devices)
    build_some(1, 0, devices)

    def transform(subgrid_slot):
        for block in range(BLOCKS):
            if block != REACH:
                rows_copy(subgrid_slot, block).wait()
        parts = [zband[subgrid_slot, block] for block in range(BLOCKS - 1)]
        parts[0] = parts[0] + zband[subgrid_slot, BLOCKS - 1]
        columns = jnp.transpose(jnp.concatenate(parts, axis=0).astype(jnp.float32))
        tiles = [
            columns[part * KC + low : part * KC + low + SUPPORT]
            for low in range(0, KC, SUPPORT)
            for part in range(2)
        ]
        turned[subgrid_slot] = jnp.concatenate(tiles, axis=0).astype(jnp.bfloat16)

    def slots_copy(place, source, target):
        return pltpu.make_async_remote_copy(
            src_ref=vsend.at[source],
            dst_ref=vrecv.at[target],
            send_sem=vs_sem.at[source],
            recv_sem=vr_sem.at[target],
            device_id={"row": place},
            device_id_type=pl.DeviceIdType.MESH,
        )

    planes = devices // PLANE

    def place_of(turn, spin):
        here = me // PLANE
        upper = here >= planes // 2
        near = jnp.where(upper, planes - 1 - here, here)
        plane = planes - turn
        plane = jnp.where(plane > near, plane, plane - 1)
        plane = jnp.where(turn == planes, near, plane)
        plane = jnp.where(upper, planes - 1 - plane, plane)
        core = me % 2
        side = me % PLANE // 2
        side = 1 - side if spin < 2 else side
        core = core if spin % 2 else 1 - core
        return plane * PLANE + side * 2 + core

    def degrid(subgrid_slot, place):
        for piece in range(share // wide):
            along = jnp.dot(
                turned[subgrid_slot],
                jnp.concatenate(
                    [
                        spreads[place, subgrid_slot, piece, group]
                        for group in range(wide // 128)
                    ],
                    axis=1,
                ),
                preferred_element_type=jnp.float32,
            )
            real = jnp.zeros((SUPPORT, wide), jnp.float32)
            imag = jnp.zeros((SUPPORT, wide), jnp.float32)
            for tile in range(KC // SUPPORT):
                low = slice(2 * tile * SUPPORT, (2 * tile + 1) * SUPPORT)
                high = slice((2 * tile + 1) * SUPPORT, (2 * tile + 2) * SUPPORT)
                factor_real = factors[place, subgrid_slot, piece, low, :]
                factor_imag = factors[place, subgrid_slot, piece, high, :]
                real = real + (along[low] * factor_real - along[high] * factor_imag)
                imag = imag + (along[low] * factor_imag + along[high] * factor_real)
            real = jnp.sum(real, axis=0, keepdims=True)
            imag = jnp.sum(imag, axis=0, keepdims=True)
            for group in range(wide // 128):
                row = piece * (wide // 128) + group
                part = slice(group * 128, (group + 1) * 128)
                first = subgrid_slot * groups + row
                found[place, first : first + 1, :] = real[:, part]
                first = (SUB_DEV + subgrid_slot) * groups + row
                found[place, first : first + 1, :] = imag[:, part]

    def send_slots(places):
        for place in places:
            vsend[place] = found[place].astype(jnp.bfloat16)
        for place in places:
            slots_copy(place, place, me).start()

    def first_pass(turn, carry):
        for spin in range(PLANE):
            degrid(0, place_of(turn, spin))
        return carry

    def second_pass(pair, carry):
        places = [
            place_of(2 * pair + turn, spin) for turn in (1, 2) for spin in range(PLANE)
        ]
        for place in places:
            degrid(1, place)
        send_slots(places)
        return carry

    transform(0)
    lax.fori_loop(1, planes, first_pass, 0, unroll=UNROLL)
    for spin in range(2):
        degrid(0, place_of(planes, spin))
    transform(1)
    lax.fori_loop(0, (planes - 2) // 2, second_pass, 0)
    nearer = [place_of(planes - 1, spin) for spin in range(PLANE)]
    nearer += [place_of(planes, spin) for spin in range(2)]
    for place in nearer:
        degrid(1, place)
    send_slots(nearer)
    beside = place_of(planes, 2)
    for subgrid_slot in range(SUB_DEV):
        degrid(subgrid_slot, beside)
        degrid(subgrid_slot, me)
    send_slots([beside])
    vrecv[me] = found[me].astype(jnp.bfloat16)

    def settle(step, carry):
        place = lax.rem(me + step, devices)
        slots_copy(place, place, place).wait()
        return carry

    lax.fori_loop(1, devices, settle, 0)
    for place in range(devices):
        taken = vrecv[place].astype(jnp.float32)
        for part in range(2):
            for subgrid_slot in range(SUB_DEV):
                for group in range(groups):
                    first = (part * SUB_DEV + subgrid_slot) * groups + group
                    row = place * SUB_DEV + subgrid_slot
                    out_ref[part, row : row + 1, group * 128 : (group + 1) * 128] = taken[
                        first : first + 1, :
                    ]


def local(
    facet_rows,
    range_start,
    range_length,
    facet_offset,
    window_table,
    kernel_table,
    cell_row,
    cell_column,
    kernel_row,
    kernel_column,
):
    devices = lax.axis_size("row")
    visibilities = cell_row.shape[1]
    share = visibilities // devices
    wide = min(256, share)
    pieces = (devices, SUB_DEV, share // wide)
    sent_rows = -(-2 * SUB_DEV * share // 128 // 16) * 16
    vmem = pl.BlockSpec(memory_space=pltpu.VMEM)
    hbm = pl.BlockSpec(memory_space=pltpu.HBM)
    operands = (
        range_start,
        range_length,
        facet_offset,
        window_table,
        facet_rows,
        kernel_table.T,
        jnp.asarray(transform_rows()),
        cell_row,
        cell_column,
        kernel_row,
        kernel_column,
    )
    return pl.pallas_call(
        functools.partial(kernel, devices, share),
        out_shape=pltpu.VMEM((2, SUB_DEV * devices, share), jnp.float32),
        in_specs=[hbm] * 11,
        out_specs=vmem,
        scratch_shapes=[
            (pltpu.SMEM if number < 3 else pltpu.VMEM)(value.shape, value.dtype)
            for number, value in enumerate(operands)
        ]
        + [
            pltpu.SemaphoreType.DMA((11,)),
            pltpu.VMEM((F // 4, LEAD + SUB + R_DEV, 128), jnp.float32),
            pltpu.VMEM((SUB_DEV, BLOCKS, R_DEV, 2 * KC), jnp.bfloat16),
            pltpu.VMEM((SUB_DEV, BLOCKS, R_DEV, 2 * KC), jnp.bfloat16),
            pltpu.VMEM((SUB_DEV, 2 * KC, SUB), jnp.bfloat16),
            pltpu.VMEM((devices, sent_rows, 128), jnp.float32),
            pltpu.VMEM((devices, sent_rows, 128), jnp.bfloat16),
            pltpu.VMEM((devices, sent_rows, 128), jnp.bfloat16),
            pltpu.VMEM(pieces + (wide // 128, SUB, 128), jnp.bfloat16),
            pltpu.VMEM(pieces + (2 * KC, wide), jnp.float32),
            pltpu.SemaphoreType.DMA((SUB_DEV, BLOCKS)),
            pltpu.SemaphoreType.DMA((SUB_DEV, BLOCKS)),
            pltpu.SemaphoreType.DMA((devices,)),
            pltpu.SemaphoreType.DMA((devices,)),
        ],
        compiler_params=pltpu.CompilerParams(
            collective_id=0, has_side_effects=True, vmem_limit_bytes=41943040
        ),
        name="extract_and_degrid",
    )(*[pltpu.with_memory_space_constraint(o, pltpu.HBM) for o in operands])


def solution(mesh):
    placed = (
        P(None, None, ("grp", "row"), None),
        P("grp"),
        P("grp"),
        P("grp"),
        P(),
        P(),
        P(("grp", "row"), None),
        P(("grp", "row"), None),
        P(("grp", "row"), None),
        P(("grp", "row"), None),
    )
    return jax.shard_map(
        local, mesh=mesh, in_specs=placed, out_specs=P(None, "grp", "row"), check_vma=False
    )
```

```python
import functools
import math

import jax
import jax.numpy as jnp
import numpy as np
from jax import lax
from jax.experimental import pallas as pl
from jax.experimental.pallas import tpu as pltpu
from jax.sharding import PartitionSpec as P

F = 16
KC = 128
SUB = 256
R_DEV = 32
SUB_DEV = 2
SUPPORT = 8
NOVER = 256
REACH = SUB // (2 * R_DEV)
BLOCKS = 2 * REACH + 1
LEAD = 160
PLANE = 4
BUILT = 8
TWO_PI = 2.0 * math.pi


def transform_rows():
    kcol = np.arange(KC)
    jcol = np.arange(SUB)
    angles = TWO_PI * (kcol[:, None] * jcol[None, :] % SUB) / SUB
    scale = 1.0 / math.sqrt(KC)
    parts = np.stack([np.cos(angles) * scale, np.sin(angles) * scale])
    tiles = parts.reshape(2, KC // SUPPORT, SUPPORT, SUB).transpose(1, 0, 2, 3)
    return tiles.reshape(2 * KC, SUB).astype(np.float32).astype(jnp.bfloat16)


def spread_taps(tables, cells, picks, turn):
    index = jnp.broadcast_to(picks, (SUPPORT, 128))
    within = index & 127
    low, high = (
        jnp.take_along_axis(table, within, axis=1, mode="promise_in_bounds") for table in tables
    )
    taps = jnp.where(index < 128, low, high)
    cell = jnp.broadcast_to(cells + turn, (SUPPORT, 128))
    for bit in (1, 2, 4):
        taps = jnp.where((cell & bit) != 0, pltpu.roll(taps, bit, axis=0), taps)
    row = lax.broadcasted_iota(jnp.int32, (SUPPORT, 128), 0)
    pick = (((cell + (SUPPORT - 1 - row)) >> 3) & (SUB // SUPPORT - 1)).astype(jnp.float32)
    pair_pick = jnp.concatenate([pick, pick - 1.0], axis=0).astype(jnp.bfloat16)
    pair_taps = jnp.concatenate([taps, taps], axis=0).astype(jnp.bfloat16)
    parts = [
        jnp.where(pair_pick == tile, pair_taps, jnp.zeros_like(pair_taps))
        for tile in range(0, SUB // SUPPORT, 2)
    ]
    return jnp.concatenate(parts, axis=0)


def kernel(
    devices,
    share,
    *refs,
):
    held = refs[:11]
    out_ref = refs[11]
    kept = refs[12:20]
    (
    starts_ref,
    lengths_ref,
    offset_ref,
    window_ref,
    rows_ref,
    table_ref,
    transform_ref,
    slots_ref,
    ) = kept
    (
    in_sem,
    windows,
    zsend,
    zband,
    turned,
    found,
    vsend,
    vrecv,
    spreads,
    factors,
    zs_sem,
    zr_sem,
    vs_sem,
    vr_sem,
    ) = refs[20:]
    cell_row_ref, cell_column_ref, kernel_row_ref, kernel_column_ref = (
        slots_ref.at[number] for number in range(4)
    )
    fetches = [
        pltpu.make_async_copy(source, target, in_sem.at[number])
        for number, (source, target) in enumerate(zip(held[:7], kept[:7]))
    ] + [
        pltpu.make_async_copy(source, slots_ref.at[number], in_sem.at[7])
        for number, source in enumerate(held[7:])
    ]
    for fetch in fetches:
        fetch.start()
    total_rows = R_DEV * devices
    me = lax.axis_index("row")
    barrier = pltpu.get_barrier_semaphore()

    def greet(step, carry):
        pl.semaphore_signal(
            barrier,
            inc=1,
            device_id={
                "row": lax.rem(me + jnp.where(me >= devices // 2, step, devices - step), devices)
            },
            device_id_type=pl.DeviceIdType.MESH,
        )
        return carry

    lax.fori_loop(1, devices, greet, 0)

    windows[:, 0:LEAD, :] = jnp.zeros((F // 4, LEAD, 128), jnp.float32)
    windows[:, LEAD + SUB :, :] = jnp.zeros((F // 4, R_DEV, 128), jnp.float32)
    for fetch in fetches[:4]:
        fetch.wait()
    for tile in range(F // 4):
        repeated = jnp.concatenate(
            [
                jnp.broadcast_to(window_ref[facet : facet + 1, :], (R_DEV, SUB))
                for facet in range(4 * tile, 4 * tile + 4)
            ],
            axis=0,
        )
        windows[tile, LEAD : LEAD + SUB, :] = jnp.transpose(repeated)
    lanes8 = lax.broadcasted_iota(jnp.int32, (8, 128), 1)
    tiles8 = lax.broadcasted_iota(jnp.int32, (8, 128), 0)
    facets8 = tiles8 * 4 + lanes8 // R_DEV
    offsets = jnp.zeros((8, 128), jnp.int32)
    for facet in range(F):
        offsets = jnp.where(facets8 == facet, offset_ref[facet], offsets)
    turns = lax.rem((me * R_DEV + lanes8 % R_DEV) * offsets, total_rows)
    angles = TWO_PI * turns.astype(jnp.float32) / total_rows
    lane_rows = lax.broadcasted_iota(jnp.int32, (R_DEV, 128), 0)
    lane_slots = lax.broadcasted_iota(jnp.int32, (R_DEV, 128), 1) % R_DEV
    diagonal = lane_rows == lane_slots

    def spread_out(values):
        return jnp.concatenate(
            [
                jnp.where(diagonal, jnp.broadcast_to(values[t : t + 1, :], (R_DEV, 128)), 0.0)
                for t in range(F // 4)
            ],
            axis=1,
        )

    cosines = spread_out(jnp.cos(angles))
    sines = spread_out(jnp.sin(angles))
    fetches[4].wait()
    held_rows = jnp.concatenate(
        [rows_ref[0].reshape(F * R_DEV, KC), rows_ref[1].reshape(F * R_DEV, KC)], axis=1
    )

    def begin_of(owner, subgrid_slot):
        start = starts_ref[owner * SUB_DEV + subgrid_slot]
        begin = lax.rem(start - owner * R_DEV + SUB // 2 + total_rows, total_rows)
        return jnp.minimum(begin, LEAD)

    def owner_of(block):
        return lax.rem(me - block + REACH + devices, devices)

    def block_sums(subgrid_slot):
        weights = []
        for block in range(BLOCKS):
            first = block * R_DEV - begin_of(owner_of(block), subgrid_slot)
            window = jnp.concatenate(
                [windows[t, pl.ds(first + LEAD, R_DEV), :] for t in range(F // 4)], axis=1
            )
            weights.append((window * cosines).astype(jnp.bfloat16))
            weights.append((window * sines).astype(jnp.bfloat16))
        sums = jnp.dot(
            jnp.concatenate(weights, axis=0), held_rows, preferred_element_type=jnp.float32
        )
        for block in range(BLOCKS):
            owner = owner_of(block)
            first = block * R_DEV - begin_of(owner, subgrid_slot)
            inside = lane_rows + first < lengths_ref[owner * SUB_DEV + subgrid_slot]
            low = block * 2 * R_DEV
            by_cosine = sums[low : low + R_DEV]
            by_sine = sums[low + R_DEV : low + 2 * R_DEV]
            real = jnp.where(inside, by_cosine[:, 0:KC] - by_sine[:, KC:], 0.0)
            imag = jnp.where(inside, by_cosine[:, KC:] + by_sine[:, 0:KC], 0.0)
            target = zband if block == REACH else zsend
            target[subgrid_slot, block, :, 0:KC] = real.astype(jnp.bfloat16)
            target[subgrid_slot, block, :, KC : 2 * KC] = imag.astype(jnp.bfloat16)

    def rows_copy(subgrid_slot, block):
        return pltpu.make_async_remote_copy(
            src_ref=zsend.at[subgrid_slot, block],
            dst_ref=zband.at[subgrid_slot, block],
            send_sem=zs_sem.at[subgrid_slot],
            recv_sem=zr_sem.at[subgrid_slot],
            device_id={"row": owner_of(block)},
            device_id_type=pl.DeviceIdType.MESH,
        )

    far_first = sorted((b for b in range(BLOCKS) if b != REACH), key=lambda b: -abs(b - REACH))
    planes = devices // PLANE
    upper = me // PLANE >= planes // 2
    edge = (me < PLANE) | (me >= devices - PLANE)

    def send_rows(subgrid_slot, steps):
        for step in steps:
            block = step if step < REACH else BLOCKS - 1 + REACH - step
            mirrored = jnp.where(upper, block, BLOCKS - 1 - block)
            rows_copy(subgrid_slot, mirrored).start()

    block_sums(0)
    pl.semaphore_wait(barrier, devices - 1)

    @pl.when(edge)
    def _():
        send_rows(0, range(REACH))

    block_sums(1)
    send_rows(0, range(REACH, 2 * REACH))

    @pl.when(jnp.logical_not(edge))
    def _():
        send_rows(0, range(REACH))

    for fetch in fetches[5:7]:
        fetch.wait()
    pltpu.make_async_copy(slots_ref, slots_ref, in_sem.at[7]).wait()
    table_low = table_ref[:, 0:128]
    table_high = table_ref[:, 128:256]
    tables = [
        part.astype(jnp.bfloat16).astype(jnp.float32) for part in (table_low, table_high)
    ]

    wide = min(256, share)
    groups = share // 128

    def build(subgrid_slot, place):
        this = pl.ds(subgrid_slot, 1)
        for piece in range(share // wide):
            lanes = [
                pl.ds(pl.multiple_of(place * share + piece * wide + at, 128), 128)
                for at in range(0, wide, 128)
            ]
            columns = [
                spread_taps(tables, cell_column_ref[this, at], kernel_column_ref[this, at], 0)
                for at in lanes
            ]
            factors[place, subgrid_slot, piece] = jnp.dot(
                transform_ref[...],
                jnp.concatenate(columns, axis=1),
                preferred_element_type=jnp.float32,
            )
            begin = begin_of(me, subgrid_slot)
            for group, at in enumerate(lanes):
                spreads[place, subgrid_slot, piece, group] = spread_taps(
                    tables, cell_row_ref[this, at], kernel_row_ref[this, at], begin
                )

    def build_some(subgrid_slot, low, high):
        def step(number, carry):
            for place in range(BUILT):
                build(subgrid_slot, number * BUILT + place)
            return carry

        lax.fori_loop(low // BUILT, high // BUILT, step, 0)

    build_some(0, 0, devices // 2)
    send_rows(1, range(2 * REACH))
    build_some(0, devices // 2, devices)
    build_some(1, 0, devices)

    def transform(subgrid_slot):
        arrived = zband.at[subgrid_slot, pl.ds(0, BLOCKS - 1)]
        pltpu.make_async_copy(arrived, arrived, zr_sem.at[subgrid_slot]).wait()
        parts = [zband[subgrid_slot, block] for block in range(BLOCKS - 1)]
        parts[0] = parts[0] + zband[subgrid_slot, BLOCKS - 1]
        columns = jnp.transpose(jnp.concatenate(parts, axis=0).astype(jnp.float32))
        tiles = [
            columns[part * KC + low : part * KC + low + SUPPORT]
            for low in range(0, KC, SUPPORT)
            for part in range(2)
        ]
        turned[subgrid_slot] = jnp.concatenate(tiles, axis=0).astype(jnp.bfloat16)

    def slots_copy(place, source, target):
        return pltpu.make_async_remote_copy(
            src_ref=vsend.at[source],
            dst_ref=vrecv.at[target],
            send_sem=vs_sem.at[0],
            recv_sem=vr_sem.at[0],
            device_id={"row": place},
            device_id_type=pl.DeviceIdType.MESH,
        )

    def place_of(turn, spin):
        here = me // PLANE
        upper = here >= planes // 2
        near = jnp.where(upper, planes - 1 - here, here)
        plane = planes - turn
        plane = jnp.where(plane > near, plane, plane - 1)
        plane = jnp.where(turn == planes, near, plane)
        plane = jnp.where(upper, planes - 1 - plane, plane)
        core = me % 2
        side = me % PLANE // 2
        side = 1 - side if spin < 2 else side
        core = core if spin % 2 else 1 - core
        return plane * PLANE + side * 2 + core

    def degrid(subgrid_slot, place):
        for piece in range(share // wide):
            along = jnp.dot(
                turned[subgrid_slot],
                jnp.concatenate(
                    [
                        spreads[place, subgrid_slot, piece, group]
                        for group in range(wide // 128)
                    ],
                    axis=1,
                ),
                preferred_element_type=jnp.float32,
            )
            real = jnp.zeros((SUPPORT, wide), jnp.float32)
            imag = jnp.zeros((SUPPORT, wide), jnp.float32)
            for tile in range(KC // SUPPORT):
                low = slice(2 * tile * SUPPORT, (2 * tile + 1) * SUPPORT)
                high = slice((2 * tile + 1) * SUPPORT, (2 * tile + 2) * SUPPORT)
                factor_real = factors[place, subgrid_slot, piece, low, :]
                factor_imag = factors[place, subgrid_slot, piece, high, :]
                real = real + (along[low] * factor_real - along[high] * factor_imag)
                imag = imag + (along[low] * factor_imag + along[high] * factor_real)
            real = jnp.sum(real, axis=0, keepdims=True)
            imag = jnp.sum(imag, axis=0, keepdims=True)
            for group in range(wide // 128):
                row = piece * (wide // 128) + group
                part = slice(group * 128, (group + 1) * 128)
                first = subgrid_slot * groups + row
                found[place, first : first + 1, :] = real[:, part]
                first = (SUB_DEV + subgrid_slot) * groups + row
                found[place, first : first + 1, :] = imag[:, part]

    def send_slots(places):
        for place in places:
            vsend[place] = found[place].astype(jnp.bfloat16)
        for place in places:
            slots_copy(place, place, me).start()

    def first_pass(turn, carry):
        for spin in range(PLANE):
            degrid(0, place_of(turn, spin))
        return carry

    def second_pass(turn, carry):
        places = [place_of(turn, spin) for spin in range(PLANE)]
        for place in places:
            degrid(1, place)
        send_slots(places)
        return carry

    transform(0)
    lax.fori_loop(1, planes, first_pass, 0, unroll=3)
    for spin in range(2):
        degrid(0, place_of(planes, spin))
    transform(1)
    lax.fori_loop(1, planes - 1, second_pass, 0)
    nearer = [place_of(planes - 1, spin) for spin in range(PLANE)]
    nearer += [place_of(planes, spin) for spin in range(2)]
    for place in nearer:
        degrid(1, place)
    send_slots(nearer)
    beside = place_of(planes, 2)
    for place in (beside, me):
        for subgrid_slot in range(SUB_DEV):
            degrid(subgrid_slot, place)
    send_slots([beside])
    vrecv[me] = found[me].astype(jnp.bfloat16)

    for subgrid_slot in range(SUB_DEV):
        gone = zsend.at[subgrid_slot, pl.ds(0, BLOCKS - 1)]
        pltpu.make_async_copy(gone, gone, zs_sem.at[subgrid_slot]).wait()
    arrived = vrecv.at[pl.ds(0, devices - 1)]
    pltpu.make_async_copy(arrived, arrived, vr_sem.at[0]).wait()
    for place in range(devices):
        taken = vrecv[place].astype(jnp.float32)
        for part in range(2):
            for subgrid_slot in range(SUB_DEV):
                for group in range(groups):
                    first = (part * SUB_DEV + subgrid_slot) * groups + group
                    row = place * SUB_DEV + subgrid_slot
                    out_ref[part, row : row + 1, group * 128 : (group + 1) * 128] = taken[
                        first : first + 1, :
                    ]
    gone = vsend.at[pl.ds(0, devices - 1)]
    pltpu.make_async_copy(gone, gone, vs_sem.at[0]).wait()


def local(
    facet_rows,
    range_start,
    range_length,
    facet_offset,
    window_table,
    kernel_table,
    cell_row,
    cell_column,
    kernel_row,
    kernel_column,
):
    devices = lax.axis_size("row")
    visibilities = cell_row.shape[1]
    share = visibilities // devices
    wide = min(256, share)
    pieces = (devices, SUB_DEV, share // wide)
    sent_rows = -(-2 * SUB_DEV * share // 128 // 16) * 16
    vmem = pl.BlockSpec(memory_space=pltpu.VMEM)
    hbm = pl.BlockSpec(memory_space=pltpu.HBM)
    operands = (
        range_start,
        range_length,
        facet_offset,
        window_table,
        facet_rows,
        kernel_table.T,
        jnp.asarray(transform_rows()),
        cell_row,
        cell_column,
        kernel_row,
        kernel_column,
    )
    return pl.pallas_call(
        functools.partial(kernel, devices, share),
        out_shape=pltpu.VMEM((2, SUB_DEV * devices, share), jnp.float32),
        in_specs=[hbm] * 11,
        out_specs=vmem,
        scratch_shapes=[
            (pltpu.SMEM if number < 3 else pltpu.VMEM)(value.shape, value.dtype)
            for number, value in enumerate(operands[:7])
        ]
        + [
            pltpu.VMEM((4,) + cell_row.shape, jnp.int32),
            pltpu.SemaphoreType.DMA((8,)),
            pltpu.VMEM((F // 4, LEAD + SUB + R_DEV, 128), jnp.float32),
            pltpu.VMEM((SUB_DEV, BLOCKS, R_DEV, 2 * KC), jnp.bfloat16),
            pltpu.VMEM((SUB_DEV, BLOCKS, R_DEV, 2 * KC), jnp.bfloat16),
            pltpu.VMEM((SUB_DEV, 2 * KC, SUB), jnp.bfloat16),
            pltpu.VMEM((devices, sent_rows, 128), jnp.float32),
            pltpu.VMEM((devices, sent_rows, 128), jnp.bfloat16),
            pltpu.VMEM((devices, sent_rows, 128), jnp.bfloat16),
            pltpu.VMEM(pieces + (wide // 128, SUB, 128), jnp.bfloat16),
            pltpu.VMEM(pieces + (2 * KC, wide), jnp.float32),
            pltpu.SemaphoreType.DMA((SUB_DEV,)),
            pltpu.SemaphoreType.DMA((SUB_DEV,)),
            pltpu.SemaphoreType.DMA((1,)),
            pltpu.SemaphoreType.DMA((1,)),
        ],
        compiler_params=pltpu.CompilerParams(
            collective_id=0, has_side_effects=True, vmem_limit_bytes=41943040
        ),
        name="extract_and_degrid",
    )(*[pltpu.with_memory_space_constraint(o, pltpu.HBM) for o in operands])


def solution(mesh):
    placed = (
        P(None, None, ("grp", "row"), None),
        P("grp"),
        P("grp"),
        P("grp"),
        P(),
        P(),
        P(("grp", "row"), None),
        P(("grp", "row"), None),
        P(("grp", "row"), None),
        P(("grp", "row"), None),
    )
    return jax.shard_map(
        local, mesh=mesh, in_specs=placed, out_specs=P(None, "grp", "row"), check_vma=False
    )
```

```python
import functools
import math

import jax
import jax.numpy as jnp
import numpy as np
from jax import lax
from jax.experimental import pallas as pl
from jax.experimental.pallas import tpu as pltpu
from jax.sharding import PartitionSpec as P

F = 16
KC = 128
SUB = 256
R_DEV = 32
SUB_DEV = 2
SUPPORT = 8
NOVER = 256
REACH = SUB // (2 * R_DEV)
BLOCKS = 2 * REACH + 1
LEAD = 160
PLANE = 4
BUILT = 8
TWO_PI = 2.0 * math.pi


def transform_rows():
    kcol = np.arange(KC)
    jcol = np.arange(SUB)
    angles = TWO_PI * (kcol[:, None] * jcol[None, :] % SUB) / SUB
    scale = 1.0 / math.sqrt(KC)
    parts = np.stack([np.cos(angles) * scale, np.sin(angles) * scale])
    tiles = parts.reshape(2, KC // SUPPORT, SUPPORT, SUB).transpose(1, 0, 2, 3)
    return tiles.reshape(2 * KC, SUB).astype(np.float32).astype(jnp.bfloat16)


def spread_taps(tables, cells, picks, turn):
    index = jnp.broadcast_to(picks, (SUPPORT, 128))
    within = index & 127
    low, high = (
        jnp.take_along_axis(table, within, axis=1, mode="promise_in_bounds") for table in tables
    )
    taps = jnp.where(index < 128, low, high)
    cell = jnp.broadcast_to(cells + turn, (SUPPORT, 128))
    for bit in (1, 2, 4):
        taps = jnp.where((cell & bit) != 0, pltpu.roll(taps, bit, axis=0), taps)
    row = lax.broadcasted_iota(jnp.int32, (SUPPORT, 128), 0)
    pick = (((cell + (SUPPORT - 1 - row)) >> 3) & (SUB // SUPPORT - 1)).astype(jnp.float32)
    pair_pick = jnp.concatenate([pick, pick - 1.0], axis=0).astype(jnp.bfloat16)
    pair_taps = jnp.concatenate([taps, taps], axis=0).astype(jnp.bfloat16)
    parts = [
        jnp.where(pair_pick == tile, pair_taps, jnp.zeros_like(pair_taps))
        for tile in range(0, SUB // SUPPORT, 2)
    ]
    return jnp.concatenate(parts, axis=0)


def kernel(
    devices,
    share,
    *refs,
):
    held = refs[:11]
    out_ref = refs[11]
    kept = refs[12:20]
    (
    starts_ref,
    lengths_ref,
    offset_ref,
    window_ref,
    rows_ref,
    table_ref,
    transform_ref,
    slots_ref,
    ) = kept
    (
    in_sem,
    windows,
    zsend,
    zband,
    turned,
    found,
    vsend,
    vrecv,
    spreads,
    factors,
    zs_sem,
    zr_sem,
    vs_sem,
    vr_sem,
    ) = refs[20:]
    cell_row_ref, cell_column_ref, kernel_row_ref, kernel_column_ref = (
        slots_ref.at[number] for number in range(4)
    )
    fetches = [
        pltpu.make_async_copy(source, target, in_sem.at[number])
        for number, (source, target) in enumerate(zip(held[:7], kept[:7]))
    ] + [
        pltpu.make_async_copy(source, slots_ref.at[number], in_sem.at[7])
        for number, source in enumerate(held[7:])
    ]
    for fetch in fetches:
        fetch.start()
    total_rows = R_DEV * devices
    me = lax.axis_index("row")
    barrier = pltpu.get_barrier_semaphore()

    close = devices <= 4 * REACH
    met = 2 * REACH if close else devices - 1

    def greet(step):
        away = jnp.where(me >= devices // 2, step, devices - step)
        pl.semaphore_signal(
            barrier,
            inc=1,
            device_id={"row": lax.rem(me + away, devices)},
            device_id_type=pl.DeviceIdType.MESH,
        )

    if close:
        for step in range(REACH, 0, -1):
            greet(step)
        for step in range(REACH, 0, -1):
            greet(devices - step)
    else:

        def greet_all(step, carry):
            greet(step)
            return carry

        lax.fori_loop(1, devices, greet_all, 0)

    windows[:, 0:LEAD, :] = jnp.zeros((F // 4, LEAD, 128), jnp.float32)
    windows[:, LEAD + SUB :, :] = jnp.zeros((F // 4, R_DEV, 128), jnp.float32)
    for fetch in fetches[:4]:
        fetch.wait()
    for tile in range(F // 4):
        repeated = jnp.concatenate(
            [
                jnp.broadcast_to(window_ref[facet : facet + 1, :], (R_DEV, SUB))
                for facet in range(4 * tile, 4 * tile + 4)
            ],
            axis=0,
        )
        windows[tile, LEAD : LEAD + SUB, :] = jnp.transpose(repeated)
    lanes8 = lax.broadcasted_iota(jnp.int32, (8, 128), 1)
    tiles8 = lax.broadcasted_iota(jnp.int32, (8, 128), 0)
    facets8 = tiles8 * 4 + lanes8 // R_DEV
    offsets = jnp.zeros((8, 128), jnp.int32)
    for facet in range(F):
        offsets = jnp.where(facets8 == facet, offset_ref[facet], offsets)
    turns = lax.rem((me * R_DEV + lanes8 % R_DEV) * offsets, total_rows)
    angles = TWO_PI * turns.astype(jnp.float32) / total_rows
    lane_rows = lax.broadcasted_iota(jnp.int32, (R_DEV, 128), 0)
    lane_slots = lax.broadcasted_iota(jnp.int32, (R_DEV, 128), 1) % R_DEV
    diagonal = lane_rows == lane_slots

    def spread_out(values):
        return jnp.concatenate(
            [
                jnp.where(diagonal, jnp.broadcast_to(values[t : t + 1, :], (R_DEV, 128)), 0.0)
                for t in range(F // 4)
            ],
            axis=1,
        )

    cosines = spread_out(jnp.cos(angles))
    sines = spread_out(jnp.sin(angles))
    fetches[4].wait()
    held_rows = jnp.concatenate(
        [rows_ref[0].reshape(F * R_DEV, KC), rows_ref[1].reshape(F * R_DEV, KC)], axis=1
    )

    def begin_of(owner, subgrid_slot):
        start = starts_ref[owner * SUB_DEV + subgrid_slot]
        begin = lax.rem(start - owner * R_DEV + SUB // 2 + total_rows, total_rows)
        return jnp.minimum(begin, LEAD)

    def owner_of(block):
        return lax.rem(me - block + REACH + devices, devices)

    def block_sums(subgrid_slot):
        weights = []
        for block in range(BLOCKS):
            first = block * R_DEV - begin_of(owner_of(block), subgrid_slot)
            window = jnp.concatenate(
                [windows[t, pl.ds(first + LEAD, R_DEV), :] for t in range(F // 4)], axis=1
            )
            weights.append((window * cosines).astype(jnp.bfloat16))
            weights.append((window * sines).astype(jnp.bfloat16))
        sums = jnp.dot(
            jnp.concatenate(weights, axis=0), held_rows, preferred_element_type=jnp.float32
        )
        for block in range(BLOCKS):
            owner = owner_of(block)
            first = block * R_DEV - begin_of(owner, subgrid_slot)
            inside = lane_rows + first < lengths_ref[owner * SUB_DEV + subgrid_slot]
            low = block * 2 * R_DEV
            by_cosine = sums[low : low + R_DEV]
            by_sine = sums[low + R_DEV : low + 2 * R_DEV]
            real = jnp.where(inside, by_cosine[:, 0:KC] - by_sine[:, KC:], 0.0)
            imag = jnp.where(inside, by_cosine[:, KC:] + by_sine[:, 0:KC], 0.0)
            target = zband if block == REACH else zsend
            target[subgrid_slot, block, :, 0:KC] = real.astype(jnp.bfloat16)
            target[subgrid_slot, block, :, KC : 2 * KC] = imag.astype(jnp.bfloat16)

    def rows_copy(subgrid_slot, block):
        return pltpu.make_async_remote_copy(
            src_ref=zsend.at[subgrid_slot, block],
            dst_ref=zband.at[subgrid_slot, block],
            send_sem=zs_sem.at[subgrid_slot],
            recv_sem=zr_sem.at[subgrid_slot],
            device_id={"row": owner_of(block)},
            device_id_type=pl.DeviceIdType.MESH,
        )

    far_first = sorted((b for b in range(BLOCKS) if b != REACH), key=lambda b: -abs(b - REACH))
    planes = devices // PLANE
    upper = me // PLANE >= planes // 2
    edge = (me < PLANE) | (me >= devices - PLANE)

    def send_rows(subgrid_slot, steps):
        for step in steps:
            block = step if step < REACH else BLOCKS - 1 + REACH - step
            mirrored = jnp.where(upper, block, BLOCKS - 1 - block)
            rows_copy(subgrid_slot, mirrored).start()

    block_sums(0)
    block_sums(1)
    pl.semaphore_wait(barrier, met)

    @pl.when(edge)
    def _():
        send_rows(0, range(REACH))

    send_rows(0, range(REACH, 2 * REACH))

    @pl.when(jnp.logical_not(edge))
    def _():
        send_rows(0, range(REACH))

    @pl.when(edge)
    def _():
        send_rows(1, range(REACH))

    for fetch in fetches[5:7]:
        fetch.wait()
    pltpu.make_async_copy(slots_ref, slots_ref, in_sem.at[7]).wait()
    table_low = table_ref[:, 0:128]
    table_high = table_ref[:, 128:256]
    tables = [
        part.astype(jnp.bfloat16).astype(jnp.float32) for part in (table_low, table_high)
    ]

    wide = min(256, share)
    groups = share // 128

    def build(subgrid_slot, place):
        this = pl.ds(subgrid_slot, 1)
        for piece in range(share // wide):
            lanes = [
                pl.ds(pl.multiple_of(place * share + piece * wide + at, 128), 128)
                for at in range(0, wide, 128)
            ]
            columns = [
                spread_taps(tables, cell_column_ref[this, at], kernel_column_ref[this, at], 0)
                for at in lanes
            ]
            product = jnp.dot(
                transform_ref[...],
                jnp.concatenate(columns, axis=1),
                preferred_element_type=jnp.float32,
            )
            for tile in range(KC // SUPPORT):
                low = 2 * tile * SUPPORT
                real = product[low : low + SUPPORT]
                imag = product[low + SUPPORT : low + 2 * SUPPORT]
                for part, value in enumerate((real, real + imag, imag - real)):
                    rows = slice((3 * tile + part) * SUPPORT, (3 * tile + part + 1) * SUPPORT)
                    factors[place, subgrid_slot, piece, rows, :] = value
            begin = begin_of(me, subgrid_slot)
            for group, at in enumerate(lanes):
                spreads[place, subgrid_slot, piece, group] = spread_taps(
                    tables, cell_row_ref[this, at], kernel_row_ref[this, at], begin
                )

    def build_some(subgrid_slot, low, high):
        def step(number, carry):
            for place in range(BUILT):
                build(subgrid_slot, number * BUILT + place)
            return carry

        lax.fori_loop(low // BUILT, high // BUILT, step, 0)

    build_some(0, 0, devices // 2)
    send_rows(1, range(REACH, 2 * REACH))

    @pl.when(jnp.logical_not(edge))
    def _():
        send_rows(1, range(REACH))

    build_some(0, devices // 2, devices)
    build_some(1, 0, devices)

    def transform(subgrid_slot):
        arrived = zband.at[subgrid_slot, pl.ds(0, BLOCKS - 1)]
        pltpu.make_async_copy(arrived, arrived, zr_sem.at[subgrid_slot]).wait()
        parts = [zband[subgrid_slot, block] for block in range(BLOCKS - 1)]
        parts[0] = parts[0] + zband[subgrid_slot, BLOCKS - 1]
        columns = jnp.transpose(jnp.concatenate(parts, axis=0).astype(jnp.float32))
        tiles = [
            columns[part * KC + low : part * KC + low + SUPPORT]
            for low in range(0, KC, SUPPORT)
            for part in range(2)
        ]
        turned[subgrid_slot] = jnp.concatenate(tiles, axis=0).astype(jnp.bfloat16)

    def slots_copy(place, source, target):
        return pltpu.make_async_remote_copy(
            src_ref=vsend.at[source],
            dst_ref=vrecv.at[target],
            send_sem=vs_sem.at[0],
            recv_sem=vr_sem.at[0],
            device_id={"row": place},
            device_id_type=pl.DeviceIdType.MESH,
        )

    def place_of(turn, spin):
        here = me // PLANE
        upper = here >= planes // 2
        near = jnp.where(upper, planes - 1 - here, here)
        plane = planes - turn
        plane = jnp.where(plane > near, plane, plane - 1)
        plane = jnp.where(turn == planes, near, plane)
        plane = jnp.where(upper, planes - 1 - plane, plane)
        core = me % 2
        side = me % PLANE // 2
        side = 1 - side if spin < 2 else side
        core = core if spin % 2 else 1 - core
        return plane * PLANE + side * 2 + core

    def degrid(subgrid_slot, place):
        for piece in range(share // wide):
            along = jnp.dot(
                turned[subgrid_slot],
                jnp.concatenate(
                    [
                        spreads[place, subgrid_slot, piece, group]
                        for group in range(wide // 128)
                    ],
                    axis=1,
                ),
                preferred_element_type=jnp.float32,
            )
            shared, from_imag, from_real = (
                jnp.zeros((SUPPORT, wide), jnp.float32) for _ in range(3)
            )
            for tile in range(KC // SUPPORT):
                low = 2 * tile * SUPPORT
                real = along[low : low + SUPPORT]
                imag = along[low + SUPPORT : low + 2 * SUPPORT]
                factor, factor_sum, factor_difference = (
                    factors[place, subgrid_slot, piece, rows, :]
                    for rows in (
                        slice((3 * tile + part) * SUPPORT, (3 * tile + part + 1) * SUPPORT)
                        for part in range(3)
                    )
                )
                shared = shared + (real + imag) * factor
                from_imag = from_imag + imag * factor_sum
                from_real = from_real + real * factor_difference
            real = shared - from_imag
            imag = shared + from_real
            real = jnp.sum(real, axis=0, keepdims=True)
            imag = jnp.sum(imag, axis=0, keepdims=True)
            for group in range(wide // 128):
                row = piece * (wide // 128) + group
                part = slice(group * 128, (group + 1) * 128)
                first = subgrid_slot * groups + row
                found[place, first : first + 1, :] = real[:, part]
                first = (SUB_DEV + subgrid_slot) * groups + row
                found[place, first : first + 1, :] = imag[:, part]

    def send_slots(places):
        for place in places:
            vsend[place] = found[place].astype(jnp.bfloat16)
        for place in places:
            slots_copy(place, place, me).start()

    def first_pass(turn, carry):
        for spin in range(PLANE):
            degrid(0, place_of(turn, spin))
        return carry

    def second_pass(turn, carry):
        places = [place_of(turn, spin) for spin in range(PLANE)]
        for place in places:
            degrid(1, place)
        send_slots(places)
        return carry

    transform(0)
    lax.fori_loop(1, planes, first_pass, 0, unroll=3)
    for spin in range(2):
        degrid(0, place_of(planes, spin))
    transform(1)
    lax.fori_loop(1, planes, second_pass, 0)
    nearer = [place_of(planes, spin) for spin in range(2)]
    for place in nearer:
        degrid(1, place)
    send_slots(nearer)
    beside = place_of(planes, 2)
    for place in (beside, me):
        for subgrid_slot in range(SUB_DEV):
            degrid(subgrid_slot, place)
    send_slots([beside])
    vrecv[me] = found[me].astype(jnp.bfloat16)

    for subgrid_slot in range(SUB_DEV):
        gone = zsend.at[subgrid_slot, pl.ds(0, BLOCKS - 1)]
        pltpu.make_async_copy(gone, gone, zs_sem.at[subgrid_slot]).wait()
    arrived = vrecv.at[pl.ds(0, devices - 1)]
    pltpu.make_async_copy(arrived, arrived, vr_sem.at[0]).wait()
    for place in range(devices):
        taken = vrecv[place].astype(jnp.float32)
        for part in range(2):
            for subgrid_slot in range(SUB_DEV):
                for group in range(groups):
                    first = (part * SUB_DEV + subgrid_slot) * groups + group
                    row = place * SUB_DEV + subgrid_slot
                    out_ref[part, row : row + 1, group * 128 : (group + 1) * 128] = taken[
                        first : first + 1, :
                    ]
    gone = vsend.at[pl.ds(0, devices - 1)]
    pltpu.make_async_copy(gone, gone, vs_sem.at[0]).wait()


def local(
    facet_rows,
    range_start,
    range_length,
    facet_offset,
    window_table,
    kernel_table,
    cell_row,
    cell_column,
    kernel_row,
    kernel_column,
):
    devices = lax.axis_size("row")
    visibilities = cell_row.shape[1]
    share = visibilities // devices
    wide = min(256, share)
    pieces = (devices, SUB_DEV, share // wide)
    sent_rows = -(-2 * SUB_DEV * share // 128 // 16) * 16
    vmem = pl.BlockSpec(memory_space=pltpu.VMEM)
    hbm = pl.BlockSpec(memory_space=pltpu.HBM)
    operands = (
        range_start,
        range_length,
        facet_offset,
        window_table,
        facet_rows,
        kernel_table.T,
        jnp.asarray(transform_rows()),
        cell_row,
        cell_column,
        kernel_row,
        kernel_column,
    )
    return pl.pallas_call(
        functools.partial(kernel, devices, share),
        out_shape=pltpu.VMEM((2, SUB_DEV * devices, share), jnp.float32),
        in_specs=[hbm] * 11,
        out_specs=vmem,
        scratch_shapes=[
            (pltpu.SMEM if number < 3 else pltpu.VMEM)(value.shape, value.dtype)
            for number, value in enumerate(operands[:7])
        ]
        + [
            pltpu.VMEM((4,) + cell_row.shape, jnp.int32),
            pltpu.SemaphoreType.DMA((8,)),
            pltpu.VMEM((F // 4, LEAD + SUB + R_DEV, 128), jnp.float32),
            pltpu.VMEM((SUB_DEV, BLOCKS, R_DEV, 2 * KC), jnp.bfloat16),
            pltpu.VMEM((SUB_DEV, BLOCKS, R_DEV, 2 * KC), jnp.bfloat16),
            pltpu.VMEM((SUB_DEV, 2 * KC, SUB), jnp.bfloat16),
            pltpu.VMEM((devices, sent_rows, 128), jnp.float32),
            pltpu.VMEM((devices, sent_rows, 128), jnp.bfloat16),
            pltpu.VMEM((devices, sent_rows, 128), jnp.bfloat16),
            pltpu.VMEM(pieces + (wide // 128, SUB, 128), jnp.bfloat16),
            pltpu.VMEM(pieces + (3 * KC, wide), jnp.float32),
            pltpu.SemaphoreType.DMA((SUB_DEV,)),
            pltpu.SemaphoreType.DMA((SUB_DEV,)),
            pltpu.SemaphoreType.DMA((1,)),
            pltpu.SemaphoreType.DMA((1,)),
        ],
        compiler_params=pltpu.CompilerParams(
            collective_id=0, has_side_effects=True, vmem_limit_bytes=52428800
        ),
        name="extract_and_degrid",
    )(*[pltpu.with_memory_space_constraint(o, pltpu.HBM) for o in operands])


def solution(mesh):
    placed = (
        P(None, None, ("grp", "row"), None),
        P("grp"),
        P("grp"),
        P("grp"),
        P(),
        P(),
        P(("grp", "row"), None),
        P(("grp", "row"), None),
        P(("grp", "row"), None),
        P(("grp", "row"), None),
    )
    return jax.shard_map(
        local, mesh=mesh, in_specs=placed, out_specs=P(None, "grp", "row"), check_vma=False
    )
```

```python
import functools
import math

import jax
import jax.numpy as jnp
import numpy as np
from jax import lax
from jax.experimental import pallas as pl
from jax.experimental.pallas import tpu as pltpu
from jax.sharding import PartitionSpec as P

F = 16
KC = 128
SUB = 256
R_DEV = 32
SUB_DEV = 2
SUPPORT = 8
NOVER = 256
REACH = SUB // (2 * R_DEV)
BLOCKS = 2 * REACH + 1
LEAD = 160
PLANE = 4
BUILT = 8
TWO_PI = 2.0 * math.pi


def transform_rows():
    kcol = np.arange(KC)
    jcol = np.arange(SUB)
    angles = TWO_PI * (kcol[:, None] * jcol[None, :] % SUB) / SUB
    scale = 1.0 / math.sqrt(KC)
    parts = np.stack([np.cos(angles) * scale, np.sin(angles) * scale])
    tiles = parts.reshape(2, KC // SUPPORT, SUPPORT, SUB).transpose(1, 0, 2, 3)
    return tiles.reshape(2 * KC, SUB).astype(np.float32).astype(jnp.bfloat16)


def spread_taps(tables, cells, picks, turn):
    index = jnp.broadcast_to(picks, (SUPPORT, 128))
    within = index & 127
    low, high = (
        jnp.take_along_axis(table, within, axis=1, mode="promise_in_bounds") for table in tables
    )
    taps = jnp.where(index < 128, low, high)
    cell = jnp.broadcast_to(cells + turn, (SUPPORT, 128))
    for bit in (1, 2, 4):
        taps = jnp.where((cell & bit) != 0, pltpu.roll(taps, bit, axis=0), taps)
    row = lax.broadcasted_iota(jnp.int32, (SUPPORT, 128), 0)
    pick = (((cell + (SUPPORT - 1 - row)) >> 3) & (SUB // SUPPORT - 1)).astype(jnp.float32)
    pair_pick = jnp.concatenate([pick, pick - 1.0], axis=0).astype(jnp.bfloat16)
    pair_taps = jnp.concatenate([taps, taps], axis=0).astype(jnp.bfloat16)
    parts = [
        jnp.where(pair_pick == tile, pair_taps, jnp.zeros_like(pair_taps))
        for tile in range(0, SUB // SUPPORT, 2)
    ]
    return jnp.concatenate(parts, axis=0)


def kernel(
    devices,
    share,
    *refs,
):
    held = refs[:11]
    out_ref = refs[11]
    kept = refs[12:20]
    (
    starts_ref,
    lengths_ref,
    offset_ref,
    window_ref,
    rows_ref,
    table_ref,
    transform_ref,
    slots_ref,
    ) = kept
    (
    in_sem,
    windows,
    zsend,
    zband,
    turned,
    found,
    vsend,
    vrecv,
    spreads,
    factors,
    zs_sem,
    zr_sem,
    vs_sem,
    vr_sem,
    ) = refs[20:]
    cell_row_ref, cell_column_ref, kernel_row_ref, kernel_column_ref = (
        slots_ref.at[number] for number in range(4)
    )
    fetches = [
        pltpu.make_async_copy(source, target, in_sem.at[number])
        for number, (source, target) in enumerate(zip(held[:7], kept[:7]))
    ] + [
        pltpu.make_async_copy(source, slots_ref.at[number], in_sem.at[7])
        for number, source in enumerate(held[7:])
    ]
    for number in (3, 0, 1, 2, 4, 5, 6, 7, 8, 9, 10):
        fetches[number].start()
    total_rows = R_DEV * devices
    me = lax.axis_index("row")
    barrier = pltpu.get_barrier_semaphore()

    close = devices <= 4 * REACH
    met = 2 * REACH if close else devices - 1

    def greet(step):
        away = jnp.where(me >= devices // 2, step, devices - step)
        pl.semaphore_signal(
            barrier,
            inc=1,
            device_id={"row": lax.rem(me + away, devices)},
            device_id_type=pl.DeviceIdType.MESH,
        )

    if close:
        for step in range(REACH, 0, -1):
            greet(step)
        for step in range(REACH, 0, -1):
            greet(devices - step)
    else:

        def greet_all(step, carry):
            greet(step)
            return carry

        lax.fori_loop(1, devices, greet_all, 0)

    windows[:, 0:LEAD, :] = jnp.zeros((F // 4, LEAD, 128), jnp.float32)
    windows[:, LEAD + SUB :, :] = jnp.zeros((F // 4, R_DEV, 128), jnp.float32)
    for fetch in fetches[:4]:
        fetch.wait()
    for tile in range(F // 4):
        repeated = jnp.concatenate(
            [
                jnp.broadcast_to(window_ref[facet : facet + 1, :], (R_DEV, SUB))
                for facet in range(4 * tile, 4 * tile + 4)
            ],
            axis=0,
        )
        windows[tile, LEAD : LEAD + SUB, :] = jnp.transpose(repeated)
    lanes8 = lax.broadcasted_iota(jnp.int32, (8, 128), 1)
    tiles8 = lax.broadcasted_iota(jnp.int32, (8, 128), 0)
    facets8 = tiles8 * 4 + lanes8 // R_DEV
    offsets = jnp.zeros((8, 128), jnp.int32)
    for facet in range(F):
        offsets = jnp.where(facets8 == facet, offset_ref[facet], offsets)
    turns = lax.rem((me * R_DEV + lanes8 % R_DEV) * offsets, total_rows)
    angles = TWO_PI * turns.astype(jnp.float32) / total_rows
    lane_rows = lax.broadcasted_iota(jnp.int32, (R_DEV, 128), 0)
    lane_slots = lax.broadcasted_iota(jnp.int32, (R_DEV, 128), 1) % R_DEV
    diagonal = lane_rows == lane_slots

    def spread_out(values):
        return jnp.concatenate(
            [
                jnp.where(diagonal, jnp.broadcast_to(values[t : t + 1, :], (R_DEV, 128)), 0.0)
                for t in range(F // 4)
            ],
            axis=1,
        )

    cosines = spread_out(jnp.cos(angles))
    sines = spread_out(jnp.sin(angles))
    fetches[4].wait()
    held_rows = jnp.concatenate(
        [rows_ref[0].reshape(F * R_DEV, KC), rows_ref[1].reshape(F * R_DEV, KC)], axis=1
    )

    def begin_of(owner, subgrid_slot):
        start = starts_ref[owner * SUB_DEV + subgrid_slot]
        begin = lax.rem(start - owner * R_DEV + SUB // 2 + total_rows, total_rows)
        return jnp.minimum(begin, LEAD)

    def owner_of(block):
        return lax.rem(me - block + REACH + devices, devices)

    def block_sums(subgrid_slot):
        weights = []
        for block in range(BLOCKS):
            first = block * R_DEV - begin_of(owner_of(block), subgrid_slot)
            window = jnp.concatenate(
                [windows[t, pl.ds(first + LEAD, R_DEV), :] for t in range(F // 4)], axis=1
            )
            weights.append((window * cosines).astype(jnp.bfloat16))
            weights.append((window * sines).astype(jnp.bfloat16))
        sums = jnp.dot(
            jnp.concatenate(weights, axis=0), held_rows, preferred_element_type=jnp.float32
        )
        for block in range(BLOCKS):
            owner = owner_of(block)
            first = block * R_DEV - begin_of(owner, subgrid_slot)
            inside = lane_rows + first < lengths_ref[owner * SUB_DEV + subgrid_slot]
            low = block * 2 * R_DEV
            by_cosine = sums[low : low + R_DEV]
            by_sine = sums[low + R_DEV : low + 2 * R_DEV]
            real = jnp.where(inside, by_cosine[:, 0:KC] - by_sine[:, KC:], 0.0)
            imag = jnp.where(inside, by_cosine[:, KC:] + by_sine[:, 0:KC], 0.0)
            target = zband if block == REACH else zsend
            target[subgrid_slot, block, :, 0:KC] = real.astype(jnp.bfloat16)
            target[subgrid_slot, block, :, KC : 2 * KC] = imag.astype(jnp.bfloat16)

    def rows_copy(subgrid_slot, block):
        return pltpu.make_async_remote_copy(
            src_ref=zsend.at[subgrid_slot, block],
            dst_ref=zband.at[subgrid_slot, block],
            send_sem=zs_sem.at[subgrid_slot],
            recv_sem=zr_sem.at[subgrid_slot],
            device_id={"row": owner_of(block)},
            device_id_type=pl.DeviceIdType.MESH,
        )

    far_first = sorted((b for b in range(BLOCKS) if b != REACH), key=lambda b: -abs(b - REACH))
    planes = devices // PLANE
    upper = me // PLANE >= planes // 2
    edge = (me < PLANE) | (me >= devices - PLANE)

    def send_rows(subgrid_slot, steps):
        for step in steps:
            block = step if step < REACH else BLOCKS - 1 + REACH - step
            mirrored = jnp.where(upper, block, BLOCKS - 1 - block)
            rows_copy(subgrid_slot, mirrored).start()

    block_sums(0)
    block_sums(1)
    for fetch in fetches[5:7]:
        fetch.wait()
    pltpu.make_async_copy(slots_ref, slots_ref, in_sem.at[7]).wait()
    table_low = table_ref[:, 0:128]
    table_high = table_ref[:, 128:256]
    tables = [
        part.astype(jnp.bfloat16).astype(jnp.float32) for part in (table_low, table_high)
    ]

    wide = min(256, share)
    groups = share // 128

    def build(subgrid_slot, place):
        this = pl.ds(subgrid_slot, 1)
        for piece in range(share // wide):
            lanes = [
                pl.ds(pl.multiple_of(place * share + piece * wide + at, 128), 128)
                for at in range(0, wide, 128)
            ]
            columns = [
                spread_taps(tables, cell_column_ref[this, at], kernel_column_ref[this, at], 0)
                for at in lanes
            ]
            product = jnp.dot(
                transform_ref[...],
                jnp.concatenate(columns, axis=1),
                preferred_element_type=jnp.float32,
            )
            for tile in range(KC // SUPPORT):
                low = 2 * tile * SUPPORT
                real = product[low : low + SUPPORT]
                imag = product[low + SUPPORT : low + 2 * SUPPORT]
                for part, value in enumerate((real, real + imag, imag - real)):
                    rows = slice((3 * tile + part) * SUPPORT, (3 * tile + part + 1) * SUPPORT)
                    factors[place, subgrid_slot, piece, rows, :] = value
            begin = begin_of(me, subgrid_slot)
            for group, at in enumerate(lanes):
                spreads[place, subgrid_slot, piece, group] = spread_taps(
                    tables, cell_row_ref[this, at], kernel_row_ref[this, at], begin
                )

    def build_some(subgrid_slot, low, high, built=BUILT):
        def step(number, carry):
            for place in range(built):
                build(subgrid_slot, number * built + place)
            return carry

        lax.fori_loop(low // built, high // built, step, 0)

    build_some(0, 0, devices // 2)
    pl.semaphore_wait(barrier, met)

    @pl.when(edge)
    def _():
        send_rows(0, range(REACH))

    send_rows(0, range(REACH, 2 * REACH))

    @pl.when(jnp.logical_not(edge))
    def _():
        send_rows(0, range(REACH))

    @pl.when(edge)
    def _():
        send_rows(1, range(REACH))

    send_rows(1, range(REACH, 2 * REACH))

    @pl.when(jnp.logical_not(edge))
    def _():
        send_rows(1, range(REACH))

    build_some(0, devices // 2, devices)
    build_some(1, 0, devices, 2 * BUILT)

    def transform(subgrid_slot):
        arrived = zband.at[subgrid_slot, pl.ds(0, BLOCKS - 1)]
        pltpu.make_async_copy(arrived, arrived, zr_sem.at[subgrid_slot]).wait()
        parts = [zband[subgrid_slot, block] for block in range(BLOCKS - 1)]
        parts[0] = parts[0] + zband[subgrid_slot, BLOCKS - 1]
        columns = jnp.transpose(jnp.concatenate(parts, axis=0).astype(jnp.float32))
        tiles = [
            columns[part * KC + low : part * KC + low + SUPPORT]
            for low in range(0, KC, SUPPORT)
            for part in range(2)
        ]
        turned[subgrid_slot] = jnp.concatenate(tiles, axis=0).astype(jnp.bfloat16)

    def slots_copy(place, source, target):
        return pltpu.make_async_remote_copy(
            src_ref=vsend.at[source],
            dst_ref=vrecv.at[target],
            send_sem=vs_sem.at[0],
            recv_sem=vr_sem.at[0],
            device_id={"row": place},
            device_id_type=pl.DeviceIdType.MESH,
        )

    def place_of(turn, spin):
        here = me // PLANE
        upper = here >= planes // 2
        near = jnp.where(upper, planes - 1 - here, here)
        plane = planes - turn
        plane = jnp.where(plane > near, plane, plane - 1)
        plane = jnp.where(turn == planes, near, plane)
        plane = jnp.where(upper, planes - 1 - plane, plane)
        core = me % 2
        side = me % PLANE // 2
        side = 1 - side if spin < 2 else side
        core = core if spin % 2 else 1 - core
        return plane * PLANE + side * 2 + core

    def degrid(subgrid_slot, place):
        for piece in range(share // wide):
            along = jnp.dot(
                turned[subgrid_slot],
                jnp.concatenate(
                    [
                        spreads[place, subgrid_slot, piece, group]
                        for group in range(wide // 128)
                    ],
                    axis=1,
                ),
                preferred_element_type=jnp.float32,
            )
            shared, from_imag, from_real = (
                jnp.zeros((SUPPORT, wide), jnp.float32) for _ in range(3)
            )
            for tile in range(KC // SUPPORT):
                low = 2 * tile * SUPPORT
                real = along[low : low + SUPPORT]
                imag = along[low + SUPPORT : low + 2 * SUPPORT]
                factor, factor_sum, factor_difference = (
                    factors[place, subgrid_slot, piece, rows, :]
                    for rows in (
                        slice((3 * tile + part) * SUPPORT, (3 * tile + part + 1) * SUPPORT)
                        for part in range(3)
                    )
                )
                shared = shared + (real + imag) * factor
                from_imag = from_imag + imag * factor_sum
                from_real = from_real + real * factor_difference
            real = shared - from_imag
            imag = shared + from_real
            real = jnp.sum(real, axis=0, keepdims=True)
            imag = jnp.sum(imag, axis=0, keepdims=True)
            for group in range(wide // 128):
                row = piece * (wide // 128) + group
                part = slice(group * 128, (group + 1) * 128)
                first = subgrid_slot * groups + row
                found[place, first : first + 1, :] = real[:, part]
                first = (SUB_DEV + subgrid_slot) * groups + row
                found[place, first : first + 1, :] = imag[:, part]

    def send_slots(places):
        for place in places:
            vsend[place] = found[place].astype(jnp.bfloat16)
        for place in places:
            slots_copy(place, place, me).start()

    def first_pass(turn, carry):
        for spin in range(PLANE):
            degrid(0, place_of(turn, spin))
        return carry

    def second_pass(turn, carry):
        places = [place_of(turn, spin) for spin in range(PLANE)]
        for place in places:
            degrid(1, place)
        send_slots(places)
        return carry

    transform(0)
    lax.fori_loop(1, planes, first_pass, 0, unroll=3)
    for spin in range(2):
        degrid(0, place_of(planes, spin))
    transform(1)
    lax.fori_loop(1, planes, second_pass, 0)
    nearer = [place_of(planes, spin) for spin in range(2)]
    for place in nearer:
        degrid(1, place)
    send_slots(nearer)
    beside = place_of(planes, 2)
    for place in (beside, me):
        for subgrid_slot in range(SUB_DEV):
            degrid(subgrid_slot, place)
    send_slots([beside])
    vrecv[me] = found[me].astype(jnp.bfloat16)

    for subgrid_slot in range(SUB_DEV):
        gone = zsend.at[subgrid_slot, pl.ds(0, BLOCKS - 1)]
        pltpu.make_async_copy(gone, gone, zs_sem.at[subgrid_slot]).wait()
    arrived = vrecv.at[pl.ds(0, devices - 1)]
    pltpu.make_async_copy(arrived, arrived, vr_sem.at[0]).wait()
    for place in range(devices):
        taken = vrecv[place].astype(jnp.float32)
        for part in range(2):
            for subgrid_slot in range(SUB_DEV):
                for group in range(groups):
                    first = (part * SUB_DEV + subgrid_slot) * groups + group
                    row = place * SUB_DEV + subgrid_slot
                    out_ref[part, row : row + 1, group * 128 : (group + 1) * 128] = taken[
                        first : first + 1, :
                    ]
    gone = vsend.at[pl.ds(0, devices - 1)]
    pltpu.make_async_copy(gone, gone, vs_sem.at[0]).wait()


def local(
    facet_rows,
    range_start,
    range_length,
    facet_offset,
    window_table,
    kernel_table,
    cell_row,
    cell_column,
    kernel_row,
    kernel_column,
):
    devices = lax.axis_size("row")
    visibilities = cell_row.shape[1]
    share = visibilities // devices
    wide = min(256, share)
    pieces = (devices, SUB_DEV, share // wide)
    sent_rows = -(-2 * SUB_DEV * share // 128 // 16) * 16
    vmem = pl.BlockSpec(memory_space=pltpu.VMEM)
    hbm = pl.BlockSpec(memory_space=pltpu.HBM)
    operands = (
        range_start,
        range_length,
        facet_offset,
        window_table,
        facet_rows,
        kernel_table.T,
        jnp.asarray(transform_rows()),
        cell_row,
        cell_column,
        kernel_row,
        kernel_column,
    )
    return pl.pallas_call(
        functools.partial(kernel, devices, share),
        out_shape=pltpu.VMEM((2, SUB_DEV * devices, share), jnp.float32),
        in_specs=[hbm] * 11,
        out_specs=vmem,
        scratch_shapes=[
            (pltpu.SMEM if number < 3 else pltpu.VMEM)(value.shape, value.dtype)
            for number, value in enumerate(operands[:7])
        ]
        + [
            pltpu.VMEM((4,) + cell_row.shape, jnp.int32),
            pltpu.SemaphoreType.DMA((8,)),
            pltpu.VMEM((F // 4, LEAD + SUB + R_DEV, 128), jnp.float32),
            pltpu.VMEM((SUB_DEV, BLOCKS, R_DEV, 2 * KC), jnp.bfloat16),
            pltpu.VMEM((SUB_DEV, BLOCKS, R_DEV, 2 * KC), jnp.bfloat16),
            pltpu.VMEM((SUB_DEV, 2 * KC, SUB), jnp.bfloat16),
            pltpu.VMEM((devices, sent_rows, 128), jnp.float32),
            pltpu.VMEM((devices, sent_rows, 128), jnp.bfloat16),
            pltpu.VMEM((devices, sent_rows, 128), jnp.bfloat16),
            pltpu.VMEM(pieces + (wide // 128, SUB, 128), jnp.bfloat16),
            pltpu.VMEM(pieces + (3 * KC, wide), jnp.float32),
            pltpu.SemaphoreType.DMA((SUB_DEV,)),
            pltpu.SemaphoreType.DMA((SUB_DEV,)),
            pltpu.SemaphoreType.DMA((1,)),
            pltpu.SemaphoreType.DMA((1,)),
        ],
        compiler_params=pltpu.CompilerParams(
            collective_id=0, has_side_effects=True, vmem_limit_bytes=52428800
        ),
        name="extract_and_degrid",
    )(*[pltpu.with_memory_space_constraint(o, pltpu.HBM) for o in operands])


def solution(mesh):
    placed = (
        P(None, None, ("grp", "row"), None),
        P("grp"),
        P("grp"),
        P("grp"),
        P(),
        P(),
        P(("grp", "row"), None),
        P(("grp", "row"), None),
        P(("grp", "row"), None),
        P(("grp", "row"), None),
    )
    return jax.shard_map(
        local, mesh=mesh, in_specs=placed, out_specs=P(None, "grp", "row"), check_vma=False
    )
```
